128 devices in a mesh: rows: 8 (over z, core), bundles: 16 (over x, y).
Axes of the slice: x: 4, y: 4, z: 4, core: 2. Of those that a mesh axis runs over, the one named last changes fastest.
Arguments:
- dense_bins: int32 [40, 16384], P(None, ('rows', 'bundles')), may hold values from 0 to 255
- bundle_bins: int32 [16384, 4096], P('rows', 'bundles'), may hold values from 0 to 255
- block_mask: int32 [128, 4096], P('rows', 'bundles'), may hold values from 0 to 1, as said below
- node_ids: int32 [16384], P(('rows', 'bundles')), may hold values from 0 to 4
- fold_ids: int32 [16384], P(('rows', 'bundles')), may hold values from 0 to 4
- grads: int32 [16384], P(('rows', 'bundles')), may hold values from -15 to 15
- hessians: int32 [16384], P(('rows', 'bundles')), may hold values from 1 to 15
Outputs:
- bundle_gain: float32 [5, 5, 4096], P(None, None, 'bundles')
- dense_gain: float32 [5, 5, 40], replicated
The draws below stay inside these ranges and needn't reach their ends.
Inputs may be any that keep to these rules, and one draw needn't show every extreme that they name: Where block_mask[i, j] is 0, rows 128 i to 128 i + 127 count in bin 0 of bundle j whatever bundle_bins holds there.
All inputs are finite; a program needn't handle non-finite values.
Results may differ from the reference program's by a relative error of at most 0.0003.
Values may be sent and summed in bfloat16 or wider, within the bound.
A program may use at most 128 MiB of HBM per device.

```python
import math
import jax
import jax.numpy as jnp
from jax import lax

BUNDLES = 4096
DENSE = 40
BINS = 256
NODES = 5
FOLDS = 5
ROWS = 16384


def draw_block_mask(key, part):
    first_key, second_key = jax.random.split(jax.random.fold_in(key, 11))
    density = jax.random.randint(first_key, (1, BUNDLES), 8, 33)
    rolled = jax.random.randint(second_key, (ROWS // 128, BUNDLES), 0, 32)
    return (rolled < density).astype(jnp.int32)


def plant(values, rng, smallest, largest):
    spot = [jax.random.randint(jax.random.fold_in(rng, axis), (), 0, length) for axis, length in enumerate(values.shape)]
    widest = values.shape.index(max(values.shape))
    beside = spot[:widest] + [(spot[widest] + 1) % values.shape[widest]] + spot[widest + 1:]
    return values.at[tuple(spot)].set(smallest).at[tuple(beside)].set(largest)


def setup_inputs(seed: int = 0) -> dict:
    key_of = jax.random.split(jax.random.key(seed), 8)
    dense_bins = plant(jax.random.randint(key_of[0], (DENSE, ROWS), 0, BINS), jax.random.fold_in(key_of[0], 1), 0, BINS - 1).astype(jnp.int32)
    bundle_bins = plant(jax.random.randint(key_of[1], (ROWS, BUNDLES), 0, BINS), jax.random.fold_in(key_of[1], 1), 0, BINS - 1).astype(jnp.int32)
    block_mask = draw_block_mask(jax.random.fold_in(key_of[7], 71), 0)
    node_ids = plant(jax.random.randint(key_of[3], (ROWS,), 0, NODES), jax.random.fold_in(key_of[3], 1), 0, NODES - 1).astype(jnp.int32)
    fold_ids = plant(jax.random.randint(key_of[4], (ROWS,), 0, FOLDS), jax.random.fold_in(key_of[4], 1), 0, FOLDS - 1).astype(jnp.int32)
    grads = plant(jax.random.randint(key_of[5], (ROWS,), -15, 16), jax.random.fold_in(key_of[5], 1), -15, 15).astype(jnp.int32)
    hessians = plant(jax.random.randint(key_of[6], (ROWS,), 1, 16), jax.random.fold_in(key_of[6], 1), 1, 15).astype(jnp.int32)
    return dict(dense_bins=dense_bins, bundle_bins=bundle_bins, block_mask=block_mask, node_ids=node_ids, fold_ids=fold_ids, grads=grads, hessians=hessians)


def gain_of(left_grad, left_hess, total_grad, total_hess):
    right_grad = total_grad - left_grad
    return (left_grad * left_grad / (left_hess + 1.0)
            + right_grad * right_grad / (total_hess - left_hess + 1.0))


def best_gain(hist):
    train = jnp.sum(hist, axis=2, keepdims=True) - hist
    left = jnp.cumsum(train, axis=-1)
    gain = gain_of(left[:, 0], left[:, 1], left[:, 0, :, :, -1:], left[:, 1, :, :, -1:])
    return jnp.max(gain[..., :-1], axis=-1).transpose(1, 2, 0)


def reference(dense_bins, bundle_bins, block_mask, node_ids, fold_ids, grads, hessians):
    pairs = FOLDS * NODES
    slot = (fold_ids * NODES + node_ids).astype(jnp.int32)
    row_data = jnp.stack([grads, hessians], -1).astype(jnp.float32)
    group = math.gcd(BUNDLES, 64)

    def bundle_block(first):
        bins = lax.dynamic_slice_in_dim(bundle_bins, first, group, 1)
        marks = jnp.repeat(lax.dynamic_slice_in_dim(block_mask, first, group, 1), 128, axis=0)
        level = jnp.where(marks > 0, bins, 0).astype(jnp.int32)
        column = jnp.arange(group, dtype=jnp.int32)[None, :]
        segment = (column * BINS + level) * pairs + slot[:, None]
        data = jnp.broadcast_to(row_data[:, None, :], (ROWS, group, 2)).reshape(-1, 2)
        summed = jax.ops.segment_sum(data, segment.reshape(-1), num_segments=group * BINS * pairs)
        return summed.reshape(group, BINS, FOLDS, NODES, 2).transpose(0, 4, 2, 3, 1)

    starts = (jnp.arange(BUNDLES // group) * group).astype(jnp.int32)
    bundle_hist = lax.map(bundle_block, starts).reshape(BUNDLES, 2, FOLDS, NODES, BINS)
    bundle_gain = best_gain(bundle_hist)

    feature = jnp.arange(DENSE, dtype=jnp.int32)[:, None]
    segment = (feature * BINS + dense_bins.astype(jnp.int32)) * pairs + slot[None, :]
    data = jnp.broadcast_to(row_data[None, :, :], (DENSE, ROWS, 2)).reshape(-1, 2)
    summed = jax.ops.segment_sum(data, segment.reshape(-1), num_segments=DENSE * BINS * pairs)
    dense_hist = summed.reshape(DENSE, BINS, FOLDS, NODES, 2).transpose(0, 4, 2, 3, 1)
    dense_gain = best_gain(dense_hist)
    return bundle_gain, dense_gain
```

```python
import jax
import jax.numpy as jnp
from jax import lax
from jax.experimental import pallas as pl
from jax.experimental.pallas import tpu as pltpu
from jax.sharding import PartitionSpec as P

NODES = 5
FOLDS = 5
PAIRS = FOLDS * NODES
NR = 8
NB = 16
DENSE = 40
PER = DENSE // NR
F32 = jnp.float32
BF16 = jnp.bfloat16


def exchange_kernel(
    bins_ref, mask_ref, dense_ref, node_ref, fold_ref, grad_ref, hess_ref,
    out_ref, meta_ref,
    level, small, gathered,
    local_sem, small_send, small_recv, bulk_send, bulk_recv, meta_send, meta_recv, dense_send, dense_recv,
):
    i = lax.axis_index("rows")
    b = lax.axis_index("bundles")
    barrier = pltpu.get_barrier_semaphore()
    for o in range(1, NR):
        pl.semaphore_signal(barrier, inc=1, device_id={"rows": lax.rem(i + o, NR)})
    for o in range(1, NB):
        pl.semaphore_signal(barrier, inc=1, device_id={"bundles": lax.rem(b + o, NB)})

    row_data = jnp.concatenate(
        [r[...].astype(F32) for r in (node_ref, fold_ref, grad_ref, hess_ref)], 0
    )
    dense = dense_ref[...].astype(F32)
    for p in range(NR):
        small[p, 0:4] = row_data
        small[p, 4 : 4 + PER] = dense[p * PER : (p + 1) * PER]

    def block(t, _):
        rows = pl.ds(pl.multiple_of(t * 128, 128), 128)
        marks = mask_ref[pl.ds(t, 1), :]
        values = jnp.where(marks > 0, bins_ref[rows, :], 0).astype(F32)
        turned = values.T.astype(BF16)
        for s in range(2):
            for p in range(NR):
                first = s * 128 + p * 16
                level[s, p, :, rows] = turned[first : first + 16]
        return 0

    lax.fori_loop(0, bins_ref.shape[0] // 128, block, 0)

    pl.semaphore_wait(barrier, NR - 1 + NB - 1)

    copies = []
    for o in range(1, NR):
        peer = lax.rem(i + o, NR)
        copy = pltpu.make_async_remote_copy(
            src_ref=small.at[peer], dst_ref=gathered.at[:, i],
            send_sem=small_send.at[o], recv_sem=small_recv.at[o], device_id={"rows": peer},
        )
        copy.start()
        copies.append(copy)
    own_small = pltpu.make_async_copy(small.at[i], gathered.at[:, i], local_sem.at[0])
    own_small.start()
    bulk = []
    for o in range(1, NR):
        peer = lax.rem(i + o, NR)
        copy = pltpu.make_async_remote_copy(
            src_ref=level.at[:, peer], dst_ref=out_ref.at[i],
            send_sem=bulk_send.at[o], recv_sem=bulk_recv.at[o], device_id={"rows": peer},
        )
        copy.start()
        bulk.append(copy)
    own_bulk = pltpu.make_async_copy(level.at[:, i], out_ref.at[i], local_sem.at[1])
    own_bulk.start()
    own_small.wait()
    for copy in copies:
        copy.wait()
    metas = []
    for o in range(1, NB):
        peer = lax.rem(b + o, NB)
        copy = pltpu.make_async_remote_copy(
            src_ref=gathered.at[0:4], dst_ref=meta_ref.at[b, 0:4],
            send_sem=meta_send.at[o], recv_sem=meta_recv.at[o], device_id={"bundles": peer},
        )
        copy.start()
        metas.append(copy)
        copy = pltpu.make_async_remote_copy(
            src_ref=gathered.at[4 + jnp.minimum(peer, PER - 1)], dst_ref=meta_ref.at[b, 4],
            send_sem=dense_send.at[o], recv_sem=dense_recv.at[o], device_id={"bundles": peer},
        )
        copy.start()
        metas.append(copy)
    own_meta = pltpu.make_async_copy(gathered.at[0:4], meta_ref.at[b, 0:4], local_sem.at[2])
    own_meta.start()
    own_dense = pltpu.make_async_copy(
        gathered.at[4 + jnp.minimum(b, PER - 1)], meta_ref.at[b, 4], local_sem.at[3]
    )
    own_dense.start()
    own_bulk.wait()
    own_meta.wait()
    own_dense.wait()
    for copy in metas:
        copy.wait()
    for copy in bulk:
        copy.wait()


def exchange(bundle_bins, block_mask, dense_bins, row_data):
    vmem = pl.BlockSpec(memory_space=pltpu.VMEM)
    rows = bundle_bins.shape[0]
    dma = pltpu.SemaphoreType.DMA
    return pl.pallas_call(
        exchange_kernel,
        out_shape=(
            jax.ShapeDtypeStruct((NR, 2, 16, rows), BF16),
            jax.ShapeDtypeStruct((NB, 5, NR, 128), F32),
        ),
        in_specs=[vmem] * 7,
        out_specs=(pl.BlockSpec(memory_space=pl.ANY), pl.BlockSpec(memory_space=pl.ANY)),
        scratch_shapes=[
            pltpu.VMEM((2, NR, 16, rows), BF16),
            pltpu.VMEM((NR, 16, 128), F32),
            pltpu.VMEM((16, NR, 128), F32),
            dma((4,)),
            dma((NR,)), dma((NR,)), dma((NR,)), dma((NR,)),
            dma((NB,)), dma((NB,)), dma((NB,)), dma((NB,)),
        ],
        compiler_params=pltpu.CompilerParams(
            collective_id=0, has_side_effects=True, vmem_limit_bytes=32 << 20
        ),
        name="exchange",
    )(bundle_bins, block_mask, dense_bins, *row_data)


def histogram_kernel(level_ref, meta_ref, out_ref, lev, weight, hist):
    rows = level_ref.shape[3]
    total = NR * rows
    chunk = 1024
    features = 33

    code = lax.broadcasted_iota(jnp.int32, (32, 128), 0)
    node_of = jnp.where(code < PAIRS, code % NODES, -1).astype(F32)
    fold_of = (code // NODES).astype(F32)

    def prepare(i, _):
        first = pl.multiple_of(i * rows, rows)
        block = level_ref[i]
        lev[0:16, pl.ds(first, rows)] = block[0].astype(F32)
        lev[16:32, pl.ds(first, rows)] = block[1].astype(F32)
        for b in range(NB):
            lanes = pl.ds(pl.multiple_of(first + b * 128, 128), 128)
            node = meta_ref[b, 0, pl.ds(i, 1), :]
            fold = meta_ref[b, 1, pl.ds(i, 1), :]
            keep = (node == node_of) & (fold != fold_of)
            for q in range(2):
                value = jnp.broadcast_to(meta_ref[b, 2 + q, pl.ds(i, 1), :], (32, 128))
                weight[q * 32 : (q + 1) * 32, lanes] = jnp.where(keep, value, 0.0).astype(BF16)
            lev[32:33, lanes] = meta_ref[b, 4, pl.ds(i, 1), :]
        return 0

    lax.fori_loop(0, NR, prepare, 0)

    def feature(j, _):
        acc = None
        for k in range(0, total, chunk):
            row = lev[pl.ds(j, 1), k : k + chunk].astype(BF16)
            high = jnp.where(row >= 128, jnp.ones((), BF16), jnp.zeros((), BF16))
            low = jnp.broadcast_to(row - high * BF16(128), (128, chunk))
            bins = lax.broadcasted_iota(jnp.int32, (128, chunk), 0).astype(BF16)
            step = jnp.where(low <= bins, jnp.ones((128, chunk), BF16), jnp.zeros((128, chunk), BF16))
            w = weight[:, k : k + chunk]
            side = jnp.broadcast_to(high, (64, chunk))
            zero = jnp.zeros((64, chunk), BF16)
            right = jnp.concatenate([jnp.where(side == 0, w, zero), jnp.where(side != 0, w, zero)], 0)
            part = lax.dot_general(step, right, (((1,), (1,)), ((), ())), preferred_element_type=F32)
            acc = part if acc is None else acc + part
        hist[j] = acc
        return 0

    lax.fori_loop(0, features, feature, 0)

    lane = lax.broadcasted_iota(jnp.int32, (128, 128), 1)
    bin_low = lax.broadcasted_iota(jnp.int32, (128, 128), 0)
    even = lane % 64 < 32
    last = (bin_low == 127) & (lane >= 64)

    def prefix(j):
        half = hist[j]
        base = jnp.broadcast_to(half[127:128], (128, 128))
        return half + jnp.where(lane >= 64, pltpu.roll(base, 64, 1), 0.0)

    def pair(p, _):
        first, second = prefix(p), prefix(p + 16)
        grad = jnp.where(even, first, pltpu.roll(second, 32, 1))
        hess = jnp.where(even, pltpu.roll(first, 96, 1), second)
        all_grad = jnp.broadcast_to(grad[127:128], (128, 128))
        all_hess = jnp.broadcast_to(hess[127:128], (128, 128))
        all_grad = jnp.where(lane >= 64, all_grad, pltpu.roll(all_grad, 64, 1))
        all_hess = jnp.where(lane >= 64, all_hess, pltpu.roll(all_hess, 64, 1))
        rest = all_grad - grad
        gain = grad * grad / (hess + 1.0) + rest * rest / (all_hess - hess + 1.0)
        best = jnp.max(jnp.where(last, -1.0, gain), 0, keepdims=True)
        best = jnp.maximum(best, pltpu.roll(best, 64, 1))
        out_ref[pl.ds(p, 1), :] = best
        return 0

    lax.fori_loop(0, 16, pair, 0)

    dense = prefix(32)
    hess = pltpu.roll(dense, 96, 1)
    all_grad = jnp.broadcast_to(pltpu.roll(dense[127:128], 64, 1), (128, 128))
    all_hess = jnp.broadcast_to(pltpu.roll(hess[127:128], 64, 1), (128, 128))
    all_grad = jnp.where(lane >= 64, dense[127:128], all_grad)
    all_hess = jnp.where(lane >= 64, hess[127:128], all_hess)
    rest = all_grad - dense
    gain = dense * dense / (hess + 1.0) + rest * rest / (all_hess - hess + 1.0)
    best = jnp.max(jnp.where(last, -1.0, gain), 0, keepdims=True)
    best = jnp.maximum(best, pltpu.roll(best, 64, 1))
    out_ref[16:24, :] = jnp.broadcast_to(best, (8, 128))


def histogram(level, meta):
    vmem = pl.BlockSpec(memory_space=pltpu.VMEM)
    total = NR * level.shape[3]
    return pl.pallas_call(
        histogram_kernel,
        out_shape=jax.ShapeDtypeStruct((24, 128), F32),
        in_specs=[vmem, vmem],
        out_specs=vmem,
        scratch_shapes=[
            pltpu.VMEM((40, total), F32),
            pltpu.VMEM((64, total), BF16),
            pltpu.VMEM((33, 128, 128), F32),
        ],
        compiler_params=pltpu.CompilerParams(vmem_limit_bytes=60 << 20),
        name="histogram",
    )(level, meta)


def gather_kernel(
    best_ref, bundle_ref, dense_ref, rows_all, dense_own, dense_all,
    local_sem, send_a, recv_a, send_b, recv_b, send_c, recv_c,
):
    i = lax.axis_index("rows")
    b = lax.axis_index("bundles")
    barrier = pltpu.get_barrier_semaphore()
    for o in range(1, NR):
        pl.semaphore_signal(barrier, inc=1, device_id={"rows": lax.rem(i + o, NR)})
    for o in range(1, NB):
        pl.semaphore_signal(barrier, inc=1, device_id={"bundles": lax.rem(b + o, NB)})
    pl.semaphore_wait(barrier, NR - 1 + NB - 1)

    def dense_copy(source, peer):
        return pltpu.make_async_remote_copy(
            src_ref=best_ref.at[pl.ds(16, 8)], dst_ref=dense_own.at[source],
            send_sem=send_a.at[peer], recv_sem=recv_a.at[source], device_id={"bundles": peer},
        )

    for source in range(PER):
        @pl.when(b == source)
        def _():
            for peer in range(NB):
                if peer != source:
                    dense_copy(source, peer).start()
            pltpu.make_async_copy(
                best_ref.at[pl.ds(16, 8)], dense_own.at[source], local_sem.at[0]
            ).start()

    copies = []
    for o in range(1, NR):
        peer = lax.rem(i + o, NR)
        copy = pltpu.make_async_remote_copy(
            src_ref=best_ref.at[pl.ds(0, 16)], dst_ref=rows_all.at[i],
            send_sem=send_b.at[o], recv_sem=recv_b.at[o], device_id={"rows": peer},
        )
        copy.start()
        copies.append(copy)
    own = pltpu.make_async_copy(best_ref.at[pl.ds(0, 16)], rows_all.at[i], local_sem.at[1])
    own.start()

    for source in range(PER):
        @pl.when(b == source)
        def _():
            pltpu.make_async_copy(
                best_ref.at[pl.ds(16, 8)], dense_own.at[source], local_sem.at[0]
            ).wait()
            for peer in range(NB):
                if peer != source:
                    dense_copy(source, peer).wait_send()

        @pl.when(b != source)
        def _():
            dense_copy(source, 0).wait_recv()

    for o in range(1, NR):
        peer = lax.rem(i + o, NR)
        copy = pltpu.make_async_remote_copy(
            src_ref=dense_own, dst_ref=dense_all.at[i],
            send_sem=send_c.at[o], recv_sem=recv_c.at[o], device_id={"rows": peer},
        )
        copy.start()
        copies.append(copy)
    own_dense = pltpu.make_async_copy(dense_own, dense_all.at[i], local_sem.at[2])
    own_dense.start()
    own.wait()
    own_dense.wait()
    for copy in copies:
        copy.wait()

    turned = rows_all[...].reshape(NR * 16, 128).T
    for k in range(FOLDS):
        bundle_ref[k, :, 0:128] = turned[k * NODES : (k + 1) * NODES]
        bundle_ref[k, :, 128:256] = turned[32 + k * NODES : 32 + (k + 1) * NODES]
    pieces = [dense_all[r, d, 0:1, :] for r in range(NR) for d in range(PER)]
    dense = jnp.concatenate(pieces + [jnp.zeros((128 - DENSE, 128), F32)], 0).T
    for k in range(FOLDS):
        dense_ref[k] = dense[k * NODES : (k + 1) * NODES, 0:DENSE]


def gather(best):
    vmem = pl.BlockSpec(memory_space=pltpu.VMEM)
    dma = pltpu.SemaphoreType.DMA
    return pl.pallas_call(
        gather_kernel,
        out_shape=(
            jax.ShapeDtypeStruct((FOLDS, NODES, 256), F32),
            jax.ShapeDtypeStruct((FOLDS, NODES, DENSE), F32),
        ),
        in_specs=[vmem],
        out_specs=(vmem, vmem),
        scratch_shapes=[
            pltpu.VMEM((NR, 16, 128), F32),
            pltpu.VMEM((PER, 8, 128), F32),
            pltpu.VMEM((NR, PER, 8, 128), F32),
            dma((3,)),
            dma((NB,)), dma((PER,)), dma((NR,)), dma((NR,)), dma((NR,)), dma((NR,)),
        ],
        compiler_params=pltpu.CompilerParams(collective_id=1, has_side_effects=True),
        name="gather",
    )(best)


def local(dense_bins, bundle_bins, block_mask, node_ids, fold_ids, grads, hessians):
    row_data = [v.reshape(1, -1) for v in (node_ids, fold_ids, grads, hessians)]
    level, meta = exchange(bundle_bins, block_mask, dense_bins, row_data)
    return gather(histogram(level, meta))


def solution(mesh):
    placed = (
        P(None, ("rows", "bundles")),
        P("rows", "bundles"),
        P("rows", "bundles"),
        P(("rows", "bundles")),
        P(("rows", "bundles")),
        P(("rows", "bundles")),
        P(("rows", "bundles")),
    )
    return jax.shard_map(
        local,
        mesh=mesh,
        in_specs=placed,
        out_specs=(P(None, None, "bundles"), P()),
        check_vma=False,
    )
```

```python
import jax
import jax.numpy as jnp
from jax import lax
from jax.experimental import pallas as pl
from jax.experimental.pallas import tpu as pltpu
from jax.sharding import PartitionSpec as P

NODES = 5
FOLDS = 5
PAIRS = FOLDS * NODES
NR = 8
NB = 16
DENSE = 40
PER = DENSE // NR
F32 = jnp.float32
BF16 = jnp.bfloat16
F8 = jnp.float8_e4m3fn
EXACT = 512.0
VMEM_BYTES = 67043328


def exchange_kernel(
    bins_hbm, mask_hbm, dense_hbm, node_hbm, fold_hbm, grad_hbm, hess_hbm,
    out_ref, meta_ref,
    bins_ref, mask_ref, dense_ref, node_ref, fold_ref, grad_ref, hess_ref, input_sem,
    level, small, gathered,
    local_sem, small_send, small_recv, bulk_send, bulk_recv, meta_send, meta_recv, dense_send, dense_recv,
):
    i = lax.axis_index("rows")
    b = lax.axis_index("bundles")
    loads = [
        pltpu.make_async_copy(source, target, input_sem.at[n])
        for n, (source, target) in enumerate(
            (
                (node_hbm, node_ref), (fold_hbm, fold_ref), (grad_hbm, grad_ref), (hess_hbm, hess_ref),
                (dense_hbm, dense_ref), (mask_hbm, mask_ref), (bins_hbm, bins_ref),
            )
        )
    ]
    for load in loads:
        load.start()
    barrier = pltpu.get_barrier_semaphore()
    for o in range(1, NR):
        pl.semaphore_signal(barrier, inc=1, device_id={"rows": lax.rem(i + o, NR)})
    for o in range(1, NB):
        pl.semaphore_signal(barrier, inc=1, device_id={"bundles": lax.rem(b + o, NB)})

    for load in loads[:5]:
        load.wait()
    row_data = jnp.concatenate(
        [r[...].astype(F32) for r in (node_ref, fold_ref, grad_ref, hess_ref)], 0
    )
    dense = dense_ref[...].astype(F32)
    for p in range(NR):
        small[p, 0:4] = row_data
        small[p, 4 : 4 + PER] = dense[p * PER : (p + 1) * PER]

    for load in loads[5:]:
        load.wait()

    def block(t, _):
        rows = pl.ds(pl.multiple_of(t * 128, 128), 128)
        marks = mask_ref[pl.ds(t, 1), :]
        values = jnp.where(marks > 0, bins_ref[rows, :], 0).astype(F32)
        turned = values.T.astype(BF16)
        for s in range(2):
            for p in range(NR):
                first = s * 128 + p * 16
                level[s, p, :, rows] = turned[first : first + 16]
        return 0

    lax.fori_loop(0, bins_ref.shape[0] // 128, block, 0)

    pl.semaphore_wait(barrier, NR - 1 + NB - 1)

    copies = []
    for o in range(1, NR):
        peer = lax.rem(i + o, NR)
        copy = pltpu.make_async_remote_copy(
            src_ref=small.at[peer], dst_ref=gathered.at[:, i],
            send_sem=small_send.at[o], recv_sem=small_recv.at[o], device_id={"rows": peer},
        )
        copy.start()
        copies.append(copy)
    own_small = pltpu.make_async_copy(small.at[i], gathered.at[:, i], local_sem.at[0])
    own_small.start()
    bulk = []
    for o in range(1, NR):
        peer = lax.rem(i + o, NR)
        copy = pltpu.make_async_remote_copy(
            src_ref=level.at[:, peer], dst_ref=out_ref.at[i],
            send_sem=bulk_send.at[o], recv_sem=bulk_recv.at[o], device_id={"rows": peer},
        )
        copy.start()
        bulk.append(copy)
    own_bulk = pltpu.make_async_copy(level.at[:, i], out_ref.at[i], local_sem.at[1])
    own_bulk.start()
    own_small.wait()
    for copy in copies:
        copy.wait()
    metas = []
    for o in range(1, NB):
        peer = lax.rem(b + o, NB)
        copy = pltpu.make_async_remote_copy(
            src_ref=gathered.at[0:4], dst_ref=meta_ref.at[b, 0:4],
            send_sem=meta_send.at[o], recv_sem=meta_recv.at[o], device_id={"bundles": peer},
        )
        copy.start()
        metas.append(copy)
        copy = pltpu.make_async_remote_copy(
            src_ref=gathered.at[4 + jnp.minimum(peer, PER - 1)], dst_ref=meta_ref.at[b, 4],
            send_sem=dense_send.at[o], recv_sem=dense_recv.at[o], device_id={"bundles": peer},
        )
        copy.start()
        metas.append(copy)
    own_meta = pltpu.make_async_copy(gathered.at[0:4], meta_ref.at[b, 0:4], local_sem.at[2])
    own_meta.start()
    own_dense = pltpu.make_async_copy(
        gathered.at[4 + jnp.minimum(b, PER - 1)], meta_ref.at[b, 4], local_sem.at[3]
    )
    own_dense.start()
    own_bulk.wait()
    own_meta.wait()
    own_dense.wait()
    for copy in metas:
        copy.wait()
    for copy in bulk:
        copy.wait()


def exchange(bundle_bins, block_mask, dense_bins, row_data):
    anywhere = pl.BlockSpec(memory_space=pl.ANY)
    rows = bundle_bins.shape[0]
    dma = pltpu.SemaphoreType.DMA
    return pl.pallas_call(
        exchange_kernel,
        out_shape=(
            jax.ShapeDtypeStruct((NR, 2, 16, rows), BF16),
            jax.ShapeDtypeStruct((NB, 5, NR, 128), F32),
        ),
        in_specs=[anywhere] * 7,
        out_specs=(anywhere, anywhere),
        scratch_shapes=[
            *(pltpu.VMEM(v.shape, v.dtype) for v in (bundle_bins, block_mask, dense_bins, *row_data)),
            dma((7,)),
            pltpu.VMEM((2, NR, 16, rows), BF16),
            pltpu.VMEM((NR, 16, 128), F32),
            pltpu.VMEM((16, NR, 128), F32),
            dma((4,)),
            dma((NR,)), dma((NR,)), dma((NR,)), dma((NR,)),
            dma((NB,)), dma((NB,)), dma((NB,)), dma((NB,)),
        ],
        compiler_params=pltpu.CompilerParams(
            collective_id=0, has_side_effects=True, vmem_limit_bytes=VMEM_BYTES
        ),
        name="exchange",
    )(bundle_bins, block_mask, dense_bins, *row_data)


def histogram_kernel(level_hbm, meta_hbm, out_ref, level_ref, meta_ref, lev, weight, hist, sems):
    rows = level_ref.shape[3]
    total = NR * rows
    chunk = 1024
    get_meta = pltpu.make_async_copy(meta_hbm, meta_ref, sems.at[0])
    get_level = pltpu.make_async_copy(level_hbm, level_ref, sems.at[1])
    get_meta.start()
    get_level.start()

    code = lax.broadcasted_iota(jnp.int32, (32, 128), 0)
    node_of = jnp.where(code < PAIRS, code % NODES, -1).astype(F32)
    fold_of = (code // NODES).astype(F32)
    get_meta.wait()

    def prepare(i, most):
        first = pl.multiple_of(i * rows, rows)
        for b in range(0, NB, 2):
            above = below = size = 0.0
            for half in range(2):
                lanes = pl.ds(pl.multiple_of(first + (b + half) * 128, 128), 128)
                node, fold, grad, hess = (
                    jnp.broadcast_to(meta_ref[b + half, n, pl.ds(i, 1), :], (32, 128)) for n in range(4)
                )
                grad = jnp.where((node == node_of) & (fold != fold_of), grad, 0.0)
                hess = jnp.where((node == node_of) & (fold == fold_of), hess, 0.0)
                weight[0:32, lanes] = grad.astype(F8)
                weight[32:64, lanes] = hess.astype(F8)
                above = above + jnp.maximum(grad, 0.0)
                below = below - jnp.minimum(grad, 0.0)
                size = size + jnp.abs(hess)
                lev[32:33, lanes] = meta_ref[b + half, 4, pl.ds(i, 1), :]
            for sizes in (above, below, size):
                most = jnp.maximum(most, jnp.sum(sizes, 1, keepdims=True))
        return most

    most = lax.fori_loop(0, NR, prepare, jnp.zeros((32, 1), F32))
    exact = jnp.max(most) <= EXACT
    get_level.wait()

    def spread(i, _):
        first = pl.multiple_of(i * rows, rows)
        lev[0:16, pl.ds(first, rows)] = level_ref[i, 0].astype(F32)
        lev[16:32, pl.ds(first, rows)] = level_ref[i, 1].astype(F32)
        return 0

    lax.fori_loop(0, NR, spread, 0)

    def feature(j, dtype):
        acc = None
        for k in range(0, total, chunk):
            row = lev[pl.ds(j, 1), k : k + chunk].astype(BF16)
            high = jnp.where(row >= 128, jnp.ones((), BF16), jnp.zeros((), BF16))
            low = jnp.broadcast_to(row - high * BF16(128), (128, chunk))
            bins = lax.broadcasted_iota(jnp.int32, (128, chunk), 0).astype(BF16)
            step = jnp.where(low <= bins, jnp.ones((128, chunk), dtype), jnp.zeros((128, chunk), dtype))
            w = weight[:, k : k + chunk].astype(dtype)
            side = jnp.broadcast_to(high, (64, chunk))
            zero = jnp.zeros((64, chunk), dtype)
            right = jnp.concatenate([jnp.where(side == 0, w, zero), jnp.where(side != 0, w, zero)], 0)
            part = lax.dot_general(step, right, (((1,), (1,)), ((), ())), preferred_element_type=F32)
            acc = part if acc is None else acc + part
        return acc

    lane = lax.broadcasted_iota(jnp.int32, (128, 128), 1)
    bin_low = lax.broadcasted_iota(jnp.int32, (128, 128), 0)
    even = lane % 64 < 32
    upper = lane >= 64
    last = (bin_low == 127) & upper

    def prefix(half):
        base = jnp.broadcast_to(pltpu.roll(half[127:128], 64, 1), (128, 128))
        return half + jnp.where(upper, base, 0.0)

    def total_of(left):
        top = left[127:128]
        return jnp.where(upper[0:1], top, pltpu.roll(top, 64, 1))

    def train_of(left):
        def from_right(v, n):
            return pltpu.roll(v, 128 - n, 1)

        folds = left + from_right(left, 5)
        folds = folds + from_right(folds, 10) + from_right(left, 20)
        folds = jnp.where(lane % 32 < NODES, folds, 0.0)
        spread = folds + pltpu.roll(folds, 5, 1)
        spread = spread + pltpu.roll(spread, 10, 1) + pltpu.roll(folds, 20, 1)
        return spread - left

    def best_of(first, second):
        first, second = prefix(first), prefix(second)
        grad = jnp.where(even, first, pltpu.roll(second, 32, 1))
        hess = train_of(jnp.where(even, pltpu.roll(first, 96, 1), second))
        rest = total_of(grad) - grad
        gain = grad * grad / (hess + 1.0) + rest * rest / (total_of(hess) - hess + 1.0)
        best = jnp.max(jnp.where(last, -1.0, gain), 0, keepdims=True)
        return jnp.maximum(best, pltpu.roll(best, 64, 1))

    def features(dtype):
        hist[...] = jnp.zeros_like(hist)

        def pair(p, _):
            out_ref[pl.ds(jnp.maximum(p - 1, 0), 1), :] = best_of(hist[0], hist[1])
            first = feature(p, dtype)
            second = feature(p + 16, dtype)
            hist[0] = first
            hist[1] = second
            return 0

        lax.fori_loop(0, 16, pair, 0)
        out_ref[15:16, :] = best_of(hist[0], hist[1])
        dense = feature(32, dtype)
        out_ref[16:24, :] = jnp.broadcast_to(best_of(dense, dense), (8, 128))

    @pl.when(exact)
    def _():
        features(F8)

    @pl.when(jnp.logical_not(exact))
    def _():
        features(BF16)


def histogram(level, meta):
    total = NR * level.shape[3]
    anywhere = pl.BlockSpec(memory_space=pl.ANY)
    return pl.pallas_call(
        histogram_kernel,
        out_shape=jax.ShapeDtypeStruct((24, 128), F32),
        in_specs=[anywhere, anywhere],
        out_specs=pl.BlockSpec(memory_space=pltpu.VMEM),
        scratch_shapes=[
            pltpu.VMEM(level.shape, BF16),
            pltpu.VMEM(meta.shape, F32),
            pltpu.VMEM((40, total), F32),
            pltpu.VMEM((64, total), F8),
            pltpu.VMEM((2, 128, 128), F32),
            pltpu.SemaphoreType.DMA((2,)),
        ],
        compiler_params=pltpu.CompilerParams(vmem_limit_bytes=VMEM_BYTES),
        name="histogram",
    )(level, meta)


def gather_kernel(
    best_ref, bundle_ref, dense_ref, rows_all, dense_own, dense_all,
    local_sem, send_a, recv_a, send_b, recv_b, send_c, recv_c,
):
    i = lax.axis_index("rows")
    b = lax.axis_index("bundles")
    barrier = pltpu.get_barrier_semaphore()
    for o in range(1, NR):
        pl.semaphore_signal(barrier, inc=1, device_id={"rows": lax.rem(i + o, NR)})
    for o in range(1, NB):
        pl.semaphore_signal(barrier, inc=1, device_id={"bundles": lax.rem(b + o, NB)})
    pl.semaphore_wait(barrier, NR - 1 + NB - 1)

    def dense_copy(source, peer):
        return pltpu.make_async_remote_copy(
            src_ref=best_ref.at[pl.ds(16, 8)], dst_ref=dense_own.at[source],
            send_sem=send_a.at[peer], recv_sem=recv_a.at[source], device_id={"bundles": peer},
        )

    for source in range(PER):
        @pl.when(b == source)
        def _():
            for peer in range(NB):
                if peer != source:
                    dense_copy(source, peer).start()
            pltpu.make_async_copy(
                best_ref.at[pl.ds(16, 8)], dense_own.at[source], local_sem.at[0]
            ).start()

    copies = []
    for o in range(1, NR):
        peer = lax.rem(i + o, NR)
        copy = pltpu.make_async_remote_copy(
            src_ref=best_ref.at[pl.ds(0, 16)], dst_ref=rows_all.at[i],
            send_sem=send_b.at[o], recv_sem=recv_b.at[o], device_id={"rows": peer},
        )
        copy.start()
        copies.append(copy)
    own = pltpu.make_async_copy(best_ref.at[pl.ds(0, 16)], rows_all.at[i], local_sem.at[1])
    own.start()

    for source in range(PER):
        @pl.when(b == source)
        def _():
            pltpu.make_async_copy(
                best_ref.at[pl.ds(16, 8)], dense_own.at[source], local_sem.at[0]
            ).wait()
            for peer in range(NB):
                if peer != source:
                    dense_copy(source, peer).wait_send()

        @pl.when(b != source)
        def _():
            dense_copy(source, 0).wait_recv()

    for o in range(1, NR):
        peer = lax.rem(i + o, NR)
        copy = pltpu.make_async_remote_copy(
            src_ref=dense_own, dst_ref=dense_all.at[i],
            send_sem=send_c.at[o], recv_sem=recv_c.at[o], device_id={"rows": peer},
        )
        copy.start()
        copies.append(copy)
    own_dense = pltpu.make_async_copy(dense_own, dense_all.at[i], local_sem.at[2])
    own_dense.start()
    own.wait()
    own_dense.wait()
    for copy in copies:
        copy.wait()

    turned = rows_all[...].reshape(NR * 16, 128).T
    for k in range(FOLDS):
        bundle_ref[k, :, 0:128] = turned[k * NODES : (k + 1) * NODES]
        bundle_ref[k, :, 128:256] = turned[32 + k * NODES : 32 + (k + 1) * NODES]
    pieces = [dense_all[r, d, 0:1, :] for r in range(NR) for d in range(PER)]
    dense = jnp.concatenate(pieces + [jnp.zeros((128 - DENSE, 128), F32)], 0).T
    for k in range(FOLDS):
        dense_ref[k] = dense[k * NODES : (k + 1) * NODES, 0:DENSE]


def gather(best):
    vmem = pl.BlockSpec(memory_space=pltpu.VMEM)
    dma = pltpu.SemaphoreType.DMA
    return pl.pallas_call(
        gather_kernel,
        out_shape=(
            jax.ShapeDtypeStruct((FOLDS, NODES, 256), F32),
            jax.ShapeDtypeStruct((FOLDS, NODES, DENSE), F32),
        ),
        in_specs=[vmem],
        out_specs=(vmem, vmem),
        scratch_shapes=[
            pltpu.VMEM((NR, 16, 128), F32),
            pltpu.VMEM((PER, 8, 128), F32),
            pltpu.VMEM((NR, PER, 8, 128), F32),
            dma((3,)),
            dma((NB,)), dma((PER,)), dma((NR,)), dma((NR,)), dma((NR,)), dma((NR,)),
        ],
        compiler_params=pltpu.CompilerParams(collective_id=1, has_side_effects=True),
        name="gather",
    )(best)


def local(dense_bins, bundle_bins, block_mask, node_ids, fold_ids, grads, hessians):
    row_data = [v.reshape(1, -1) for v in (node_ids, fold_ids, grads, hessians)]
    level, meta = exchange(bundle_bins, block_mask, dense_bins, row_data)
    return gather(histogram(level, meta))


def solution(mesh):
    placed = (
        P(None, ("rows", "bundles")),
        P("rows", "bundles"),
        P("rows", "bundles"),
        P(("rows", "bundles")),
        P(("rows", "bundles")),
        P(("rows", "bundles")),
        P(("rows", "bundles")),
    )
    return jax.shard_map(
        local,
        mesh=mesh,
        in_specs=placed,
        out_specs=(P(None, None, "bundles"), P()),
        check_vma=False,
    )
```

```python
import functools

import jax
import jax.numpy as jnp
from jax import lax
from jax.experimental import pallas as pl
from jax.experimental.pallas import tpu as pltpu
from jax.sharding import PartitionSpec as P

NODES = 5
FOLDS = 5
PAIRS = FOLDS * NODES
NR = 8
NB = 16
DENSE = 40
PER = DENSE // NR
PIECES = 4
EARLY = 2
F32 = jnp.float32
BF16 = jnp.bfloat16
F8 = jnp.float8_e4m3fn
EXACT = 512.0
VMEM_BYTES = 67043328


def lanes_of():
    return lax.broadcasted_iota(jnp.int32, (128, 128), 1)


def prefix(half):
    base = jnp.broadcast_to(pltpu.roll(half[127:128], 64, 1), (128, 128))
    return half + jnp.where(lanes_of() >= 64, base, 0.0)


def total_of(left):
    top = left[127:128]
    return jnp.where(lanes_of()[0:1] >= 64, top, pltpu.roll(top, 64, 1))


def train_of(left):
    def from_right(v, n):
        return pltpu.roll(v, 128 - n, 1)

    folds = left + from_right(left, 5)
    folds = folds + from_right(folds, 10) + from_right(left, 20)
    folds = jnp.where(lanes_of() % 32 < NODES, folds, 0.0)
    spread = folds + pltpu.roll(folds, 5, 1)
    spread = spread + pltpu.roll(spread, 10, 1) + pltpu.roll(folds, 20, 1)
    return spread - left


def best_of(first, second):
    lane = lanes_of()
    last = (lax.broadcasted_iota(jnp.int32, (128, 128), 0) == 127) & (lane >= 64)
    even = lane % 64 < 32
    first, second = prefix(first), prefix(second)
    grad = jnp.where(even, first, pltpu.roll(second, 32, 1))
    hess = train_of(jnp.where(even, pltpu.roll(first, 96, 1), second))
    rest = total_of(grad) - grad
    gain = grad * grad / (hess + 1.0) + rest * rest / (total_of(hess) - hess + 1.0)
    best = jnp.max(jnp.where(last, -1.0, gain), 0, keepdims=True)
    return jnp.maximum(best, pltpu.roll(best, 64, 1))


def sums_of(row, w, dtype):
    rows = row.shape[1]
    high = jnp.where(row >= 128, jnp.ones((), BF16), jnp.zeros((), BF16))
    low = jnp.broadcast_to(row - high * BF16(128), (128, rows))
    bins = lax.broadcasted_iota(jnp.int32, (128, rows), 0).astype(BF16)
    step = jnp.where(low <= bins, jnp.ones((128, rows), dtype), jnp.zeros((128, rows), dtype))
    side = jnp.broadcast_to(high, (64, rows))
    zero = jnp.zeros((64, rows), dtype)
    right = jnp.concatenate([jnp.where(side == 0, w, zero), jnp.where(side != 0, w, zero)], 0)
    return lax.dot_general(step, right, (((1,), (1,)), ((), ())), preferred_element_type=F32)


def exchange_kernel(
    bins_hbm, mask_hbm, dense_hbm, node_hbm, fold_hbm, grad_hbm, hess_hbm,
    out_ref, weight_out, most_out, dense_out,
    bins_ref, mask_ref, dense_ref, node_ref, fold_ref, grad_ref, hess_ref, input_sem,
    level, small, gathered, kinds, meta_ref, weight, most_ref, best,
    local_sem, weight_sem, small_send, small_recv, bulk_send, bulk_recv, meta_send, meta_recv, dense_send, dense_recv,
):
    i = lax.axis_index("rows")
    b = lax.axis_index("bundles")
    loads = [
        pltpu.make_async_copy(source, target, input_sem.at[n])
        for n, (source, target) in enumerate(
            (
                (node_hbm, node_ref), (fold_hbm, fold_ref), (grad_hbm, grad_ref), (hess_hbm, hess_ref),
                (dense_hbm, dense_ref), (mask_hbm, mask_ref),
            )
        )
    ]
    piece_rows = bins_ref.shape[0] // PIECES
    bins_loads = [
        pltpu.make_async_copy(
            bins_hbm.at[pl.ds(n * piece_rows, piece_rows)],
            bins_ref.at[pl.ds(n * piece_rows, piece_rows)],
            input_sem.at[6 + n],
        )
        for n in range(PIECES)
    ]
    for load in loads + bins_loads:
        load.start()
    barrier = pltpu.get_barrier_semaphore()
    for o in range(1, NR):
        pl.semaphore_signal(barrier, inc=1, device_id={"rows": lax.rem(i + o, NR)})
    for o in range(1, NB):
        pl.semaphore_signal(barrier, inc=1, device_id={"bundles": lax.rem(b + o, NB)})

    def turn_piece(piece):
        bins_loads[piece].wait()

        def block(t, _):
            rows = pl.ds(pl.multiple_of(t * 128, 128), 128)
            marks = mask_ref[pl.ds(t, 1), :]
            values = jnp.where(marks > 0, bins_ref[rows, :], 0).astype(F32)
            turned = values.T.astype(BF16)
            for s in range(2):
                for p in range(NR):
                    first = s * 128 + p * 16
                    level[s, p, :, rows] = turned[first : first + 16]
            return 0

        blocks = piece_rows // 128
        lax.fori_loop(piece * blocks, (piece + 1) * blocks, block, 0)

    def send_piece(piece):
        lanes = pl.ds(piece * piece_rows, piece_rows)
        for o in range(1, NR):
            peer = lax.rem(i + o, NR)
            copy = pltpu.make_async_remote_copy(
                src_ref=level.at[:, peer, :, lanes], dst_ref=out_ref.at[i, :, :, lanes],
                send_sem=bulk_send.at[piece, o], recv_sem=bulk_recv.at[piece, o],
                device_id={"rows": peer},
            )
            copy.start()
            bulk.append(copy)

    for load in loads[:5]:
        load.wait()
    row_data = jnp.concatenate(
        [r[...].astype(F32) for r in (node_ref, fold_ref, grad_ref, hess_ref)], 0
    )
    dense = dense_ref[...].astype(F32)
    for p in range(NR):
        small[p, 0:4] = row_data
        small[p, 4 : 4 + PER] = dense[p * PER : (p + 1) * PER]

    loads[5].wait()
    for piece in range(EARLY):
        turn_piece(piece)
    pl.semaphore_wait(barrier, NR - 1 + NB - 1)

    copies = []
    for o in range(1, NR):
        peer = lax.rem(i + o, NR)
        copy = pltpu.make_async_remote_copy(
            src_ref=small.at[peer], dst_ref=gathered.at[i],
            send_sem=small_send.at[o], recv_sem=small_recv.at[o], device_id={"rows": peer},
        )
        copy.start()
        copies.append(copy)
    own_small = pltpu.make_async_copy(small.at[i], gathered.at[i], local_sem.at[0])
    own_small.start()

    bulk = []
    for piece in range(EARLY):
        send_piece(piece)
    own_small.wait()
    for copy in copies:
        copy.wait()
    for n in range(4 + PER):
        kinds[n] = jnp.concatenate([gathered[p, n : n + 1, :] for p in range(NR)], 0)
    metas = []
    for o in range(1, NB):
        peer = lax.rem(b + o, NB)
        copy = pltpu.make_async_remote_copy(
            src_ref=kinds.at[0:4], dst_ref=meta_ref.at[b, 0:4],
            send_sem=meta_send.at[o], recv_sem=meta_recv.at[o], device_id={"bundles": peer},
        )
        copy.start()
        metas.append(copy)
        copy = pltpu.make_async_remote_copy(
            src_ref=kinds.at[4 + jnp.minimum(peer, PER - 1)], dst_ref=meta_ref.at[b, 4],
            send_sem=dense_send.at[o], recv_sem=dense_recv.at[o], device_id={"bundles": peer},
        )
        copy.start()
        metas.append(copy)
    own_meta = pltpu.make_async_copy(kinds.at[0:4], meta_ref.at[b, 0:4], local_sem.at[2])
    own_meta.start()
    own_dense = pltpu.make_async_copy(
        kinds.at[4 + jnp.minimum(b, PER - 1)], meta_ref.at[b, 4], local_sem.at[3]
    )
    own_dense.start()
    for piece in range(EARLY, PIECES):
        turn_piece(piece)
        send_piece(piece)
    own_bulk = pltpu.make_async_copy(level.at[:, i], out_ref.at[i], local_sem.at[1])
    own_bulk.start()
    own_meta.wait()
    own_dense.wait()
    for copy in metas:
        copy.wait()

    code = lax.broadcasted_iota(jnp.int32, (32, 128), 0)
    node_of = jnp.where(code < PAIRS, code % NODES, -1).astype(F32)
    fold_of = (code // NODES).astype(F32)
    rows = bins_ref.shape[0]

    def weights_out(p):
        lanes = pl.ds(pl.multiple_of(p * rows, rows), rows)
        return pltpu.make_async_copy(weight.at[:, lanes], weight_out.at[:, lanes], weight_sem.at[p])

    def prepare(p, carry):
        most, dense = carry
        first = pl.multiple_of(p * rows, rows)
        for n in range(0, NB, 2):
            above = below = size = 0.0
            for half in range(2):
                lanes = pl.ds(pl.multiple_of(first + (n + half) * 128, 128), 128)
                node, fold, grad, hess = (
                    jnp.broadcast_to(meta_ref[n + half, m, pl.ds(p, 1), :], (32, 128)) for m in range(4)
                )
                grad = jnp.where((node == node_of) & (fold != fold_of), grad, 0.0)
                hess = jnp.where((node == node_of) & (fold == fold_of), hess, 0.0)
                weight[0:32, lanes] = grad.astype(BF16)
                weight[32:64, lanes] = hess.astype(BF16)
                above = above + jnp.maximum(grad, 0.0)
                below = below - jnp.minimum(grad, 0.0)
                size = size + jnp.abs(hess)
            for sizes in (above, below, size):
                most = jnp.maximum(most, jnp.sum(sizes, 1, keepdims=True))
        row = jnp.concatenate([meta_ref[n, 4, pl.ds(p, 1), :] for n in range(NB)], 1).astype(BF16)
        w = weight[:, pl.ds(first, rows)]
        weights_out(p).start()
        return most, dense + sums_of(row, w, BF16)

    most, dense = lax.fori_loop(
        0, NR, prepare, (jnp.zeros((32, 1), F32), jnp.zeros((128, 128), F32))
    )
    most_ref[...] = jnp.broadcast_to(most, (32, 128))
    best[...] = jnp.broadcast_to(best_of(dense, dense), (8, 128))
    own_most = pltpu.make_async_copy(most_ref, most_out, local_sem.at[4])
    own_most.start()

    own_best = pltpu.make_async_copy(best, dense_out, local_sem.at[5])
    own_best.start()
    own_bulk.wait()
    own_most.wait()
    for p in range(NR):
        weights_out(p).wait()
    for copy in bulk:
        copy.wait()
    own_best.wait()


def exchange(bundle_bins, block_mask, dense_bins, row_data):
    anywhere = pl.BlockSpec(memory_space=pl.ANY)
    rows = bundle_bins.shape[0]
    dma = pltpu.SemaphoreType.DMA
    return pl.pallas_call(
        exchange_kernel,
        out_shape=(
            jax.ShapeDtypeStruct((NR, 2, 16, rows), BF16),
            jax.ShapeDtypeStruct((64, NR * rows), BF16),
            jax.ShapeDtypeStruct((32, 128), F32),
            jax.ShapeDtypeStruct((8, 128), F32),
        ),
        in_specs=[anywhere] * 7,
        out_specs=(anywhere,) * 4,
        scratch_shapes=[
            *(pltpu.VMEM(v.shape, v.dtype) for v in (bundle_bins, block_mask, dense_bins, *row_data)),
            dma((6 + PIECES,)),
            pltpu.VMEM((2, NR, 16, rows), BF16),
            pltpu.VMEM((NR, 16, 128), F32),
            pltpu.VMEM((NR, 16, 128), F32),
            pltpu.VMEM((4 + PER, NR, 128), F32),
            pltpu.VMEM((NB, 5, NR, 128), F32),
            pltpu.VMEM((64, NR * rows), BF16),
            pltpu.VMEM((32, 128), F32),
            pltpu.VMEM((8, 128), F32),
            dma((6,)), dma((NR,)),
            dma((NR,)), dma((NR,)), dma((PIECES, NR)), dma((PIECES, NR)),
            dma((NB,)), dma((NB,)), dma((NB,)), dma((NB,)),
        ],
        compiler_params=pltpu.CompilerParams(
            collective_id=0, has_side_effects=True, vmem_limit_bytes=VMEM_BYTES
        ),
        name="exchange",
    )(bundle_bins, block_mask, dense_bins, *row_data)


def finish_kernel(
    narrow, level_hbm, weight_hbm, dense_hbm, bundle_ref, dense_ref,
    level_ref, wide, dense_best, lev, weight, hist, best, rows_all, dense_own, dense_all,
    sems, send_a, recv_a, send_b, recv_b, send_c, recv_c,
):
    i = lax.axis_index("rows")
    b = lax.axis_index("bundles")
    rows = level_ref.shape[3]
    total = NR * rows
    chunk = 1024
    dtype = F8 if narrow else BF16
    loads = [
        pltpu.make_async_copy(source, target, sems.at[n])
        for n, (source, target) in enumerate(
            ((level_hbm, level_ref), (weight_hbm, wide), (dense_hbm, dense_best))
        )
    ]
    for load in loads:
        load.start()
    barrier = pltpu.get_barrier_semaphore()
    for o in range(1, NR):
        pl.semaphore_signal(barrier, inc=1, device_id={"rows": lax.rem(i + o, NR)})
    for o in range(1, NB):
        pl.semaphore_signal(barrier, inc=1, device_id={"bundles": lax.rem(b + o, NB)})

    loads[0].wait()

    def spread(p, _):
        first = pl.multiple_of(p * rows, rows)
        lev[0:16, pl.ds(first, rows)] = level_ref[p, 0].astype(F32)
        lev[16:32, pl.ds(first, rows)] = level_ref[p, 1].astype(F32)
        return 0

    lax.fori_loop(0, NR, spread, 0)
    loads[1].wait()
    loads[2].wait()
    if narrow:
        def convert(p, _):
            lanes = pl.ds(pl.multiple_of(p * rows, rows), rows)
            weight[:, lanes] = wide[:, lanes].astype(F8)
            return 0

        lax.fori_loop(0, NR, convert, 0)

    def feature(j):
        acc = None
        for k in range(0, total, chunk):
            w = (weight if narrow else wide)[:, k : k + chunk]
            part = sums_of(lev[pl.ds(j, 1), k : k + chunk].astype(BF16), w, dtype)
            acc = part if acc is None else acc + part
        return acc

    def across(source, peer):
        return pltpu.make_async_remote_copy(
            src_ref=dense_best, dst_ref=dense_own.at[source],
            send_sem=send_a.at[peer], recv_sem=recv_a.at[source], device_id={"bundles": peer},
        )

    def own_across(source):
        return pltpu.make_async_copy(dense_best, dense_own.at[source], sems.at[3])

    def along(o, source, target, send, recv):
        return pltpu.make_async_remote_copy(
            src_ref=source, dst_ref=target.at[i],
            send_sem=send.at[o], recv_sem=recv.at[o], device_id={"rows": lax.rem(i + o, NR)},
        )

    hist[...] = jnp.zeros_like(hist)

    def pair(p, _):
        @pl.when(p == 3)
        def _():
            pl.semaphore_wait(barrier, NR - 1 + NB - 1)
            for source in range(PER):
                @pl.when(b == source)
                def _():
                    for peer in range(NB):
                        if peer != source:
                            across(source, peer).start()
                    own_across(source).start()

        @pl.when(p == 10)
        def _():
            for source in range(PER):
                @pl.when(b == source)
                def _():
                    own_across(source).wait()
                    for peer in range(NB):
                        if peer != source:
                            across(source, peer).wait_send()

                @pl.when(b != source)
                def _():
                    across(source, 0).wait_recv()
            for o in range(1, NR):
                along(o, dense_own, dense_all, send_c, recv_c).start()
            pltpu.make_async_copy(dense_own, dense_all.at[i], sems.at[4]).start()

        best[pl.ds(jnp.maximum(p - 1, 0), 1), :] = best_of(hist[0], hist[1])
        first = feature(p)
        second = feature(p + 16)
        hist[0] = first
        hist[1] = second
        return 0

    lax.fori_loop(0, 16, pair, 0)
    best[15:16, :] = best_of(hist[0], hist[1])

    pltpu.make_async_copy(dense_own, dense_all.at[i], sems.at[4]).wait()
    for o in range(1, NR):
        along(o, dense_own, dense_all, send_c, recv_c).wait()
    for o in range(1, NR):
        along(o, best, rows_all, send_b, recv_b).start()
    own = pltpu.make_async_copy(best, rows_all.at[i], sems.at[5])
    own.start()
    pieces = [dense_all[r, d, 0:1, :] for r in range(NR) for d in range(PER)]
    dense = jnp.concatenate(pieces + [jnp.zeros((128 - DENSE, 128), F32)], 0).T
    for k in range(FOLDS):
        dense_ref[k] = dense[k * NODES : (k + 1) * NODES, 0:DENSE]
    own.wait()
    for o in range(1, NR):
        along(o, best, rows_all, send_b, recv_b).wait()
    turned = rows_all[...].reshape(NR * 16, 128).T
    for k in range(FOLDS):
        bundle_ref[k, :, 0:128] = turned[k * NODES : (k + 1) * NODES]
        bundle_ref[k, :, 128:256] = turned[32 + k * NODES : 32 + (k + 1) * NODES]


def finish(narrow, level, weight, dense):
    anywhere = pl.BlockSpec(memory_space=pl.ANY)
    vmem = pl.BlockSpec(memory_space=pltpu.VMEM)
    dma = pltpu.SemaphoreType.DMA
    return pl.pallas_call(
        functools.partial(finish_kernel, narrow),
        out_shape=(
            jax.ShapeDtypeStruct((FOLDS, NODES, 256), F32),
            jax.ShapeDtypeStruct((FOLDS, NODES, DENSE), F32),
        ),
        in_specs=[anywhere] * 3,
        out_specs=(vmem, vmem),
        scratch_shapes=[
            pltpu.VMEM(level.shape, BF16),
            pltpu.VMEM(weight.shape, BF16),
            pltpu.VMEM((8, 128), F32),
            pltpu.VMEM((32, weight.shape[1]), F32),
            pltpu.VMEM(weight.shape if narrow else (32, 128), F8),
            pltpu.VMEM((2, 128, 128), F32),
            pltpu.VMEM((16, 128), F32),
            pltpu.VMEM((NR, 16, 128), F32),
            pltpu.VMEM((PER, 8, 128), F32),
            pltpu.VMEM((NR, PER, 8, 128), F32),
            dma((6,)), dma((NB,)), dma((PER,)), dma((NR,)), dma((NR,)), dma((NR,)), dma((NR,)),
        ],
        compiler_params=pltpu.CompilerParams(
            collective_id=1 if narrow else 2, has_side_effects=True, vmem_limit_bytes=VMEM_BYTES
        ),
        name="finish8" if narrow else "finish16",
    )(level, weight, dense)


def local(dense_bins, bundle_bins, block_mask, node_ids, fold_ids, grads, hessians):
    row_data = [v.reshape(1, -1) for v in (node_ids, fold_ids, grads, hessians)]
    level, weight, most, dense = exchange(bundle_bins, block_mask, dense_bins, row_data)
    return lax.cond(
        jnp.max(most) <= EXACT,
        functools.partial(finish, True), functools.partial(finish, False),
        level, weight, dense,
    )


def solution(mesh):
    placed = (
        P(None, ("rows", "bundles")),
        P("rows", "bundles"),
        P("rows", "bundles"),
        P(("rows", "bundles")),
        P(("rows", "bundles")),
        P(("rows", "bundles")),
        P(("rows", "bundles")),
    )
    return jax.shard_map(
        local,
        mesh=mesh,
        in_specs=placed,
        out_specs=(P(None, None, "bundles"), P()),
        check_vma=False,
    )
```

```python
import functools

import jax
import jax.numpy as jnp
from jax import lax
from jax.experimental import pallas as pl
from jax.experimental.pallas import tpu as pltpu
from jax.sharding import PartitionSpec as P

NODES = 5
FOLDS = 5
PAIRS = FOLDS * NODES
NR = 8
NB = 16
DENSE = 40
PER = DENSE // NR
PIECES = 2
EARLY = 1
F32 = jnp.float32
BF16 = jnp.bfloat16
F8 = jnp.float8_e4m3fn
EXACT = 512.0
VMEM_BYTES = 67043328


def lanes_of():
    return lax.broadcasted_iota(jnp.int32, (128, 128), 1)


def prefix(half):
    base = jnp.broadcast_to(pltpu.roll(half[127:128], 64, 1), (128, 128))
    return half + jnp.where(lanes_of() >= 64, base, 0.0)


def total_of(left):
    top = left[127:128]
    return jnp.where(lanes_of()[0:1] >= 64, top, pltpu.roll(top, 64, 1))


def train_of(left):
    def from_right(v, n):
        return pltpu.roll(v, 128 - n, 1)

    folds = left + from_right(left, 5)
    folds = folds + from_right(folds, 10) + from_right(left, 20)
    folds = jnp.where(lanes_of() % 32 < NODES, folds, 0.0)
    spread = folds + pltpu.roll(folds, 5, 1)
    spread = spread + pltpu.roll(spread, 10, 1) + pltpu.roll(folds, 20, 1)
    return spread - left


def best_of(first, second):
    lane = lanes_of()
    last = (lax.broadcasted_iota(jnp.int32, (128, 128), 0) == 127) & (lane >= 64)
    even = lane % 64 < 32
    first, second = prefix(first), prefix(second)
    grad = jnp.where(even, first, pltpu.roll(second, 32, 1))
    hess = train_of(jnp.where(even, pltpu.roll(first, 96, 1), second))
    rest = total_of(grad) - grad
    gain = grad * grad / (hess + 1.0) + rest * rest / (total_of(hess) - hess + 1.0)
    best = jnp.max(jnp.where(last, -1.0, gain), 0, keepdims=True)
    return jnp.maximum(best, pltpu.roll(best, 64, 1))


def sums_of(row, w, dtype):
    rows = row.shape[1]
    high = jnp.where(row >= 128, jnp.ones((), BF16), jnp.zeros((), BF16))
    low = jnp.broadcast_to(row - high * BF16(128), (128, rows))
    bins = lax.broadcasted_iota(jnp.int32, (128, rows), 0).astype(BF16)
    step = jnp.where(low <= bins, jnp.ones((128, rows), dtype), jnp.zeros((128, rows), dtype))
    side = jnp.broadcast_to(high, (64, rows))
    zero = jnp.zeros((64, rows), dtype)
    right = jnp.concatenate([jnp.where(side == 0, w, zero), jnp.where(side != 0, w, zero)], 0)
    return lax.dot_general(step, right, (((1,), (1,)), ((), ())), preferred_element_type=F32)


def exchange_kernel(
    bins_hbm, mask_hbm, dense_hbm, node_hbm, fold_hbm, grad_hbm, hess_hbm,
    out_ref, weight_out, most_out, dense_out,
    bins_ref, mask_ref, dense_ref, node_ref, fold_ref, grad_ref, hess_ref, input_sem,
    level, small, gathered, kinds, meta_ref, rows_of, weight, most_ref, dense_row,
    local_sem, weight_sem, small_send, small_recv, bulk_send, bulk_recv, meta_send, meta_recv, dense_send, dense_recv,
):
    i = lax.axis_index("rows")
    b = lax.axis_index("bundles")
    barrier = pltpu.get_barrier_semaphore()
    for o in range(1, NR):
        pl.semaphore_signal(barrier, inc=1, device_id={"rows": lax.rem(i + o, NR)})
    for o in range(1, NB):
        pl.semaphore_signal(barrier, inc=1, device_id={"bundles": lax.rem(b + o, NB)})
    loads = [
        pltpu.make_async_copy(source, target, input_sem.at[n])
        for n, (source, target) in enumerate(
            (
                (node_hbm, node_ref), (fold_hbm, fold_ref), (grad_hbm, grad_ref), (hess_hbm, hess_ref),
                (dense_hbm, dense_ref), (mask_hbm, mask_ref),
            )
        )
    ]
    piece_rows = bins_ref.shape[0] // PIECES
    bins_loads = [
        pltpu.make_async_copy(
            bins_hbm.at[pl.ds(n * piece_rows, piece_rows)],
            bins_ref.at[pl.ds(n * piece_rows, piece_rows)],
            input_sem.at[6 + n],
        )
        for n in range(PIECES)
    ]
    for load in loads + bins_loads:
        load.start()

    def turn_piece(piece):
        bins_loads[piece].wait()

        def block(t, _):
            rows = pl.ds(pl.multiple_of(t * 128, 128), 128)
            marks = mask_ref[pl.ds(t, 1), :]
            values = jnp.where(marks > 0, bins_ref[rows, :], 0).astype(F32)
            turned = values.T.astype(BF16)
            for s in range(2):
                for p in range(NR):
                    first = s * 128 + p * 16
                    level[s, p, :, rows] = turned[first : first + 16]
            return 0

        blocks = piece_rows // 128
        lax.fori_loop(piece * blocks, (piece + 1) * blocks, block, 0)

    def send_piece(piece):
        lanes = pl.ds(piece * piece_rows, piece_rows)
        for o in range(1, NR):
            peer = lax.rem(i + o, NR)
            copy = pltpu.make_async_remote_copy(
                src_ref=level.at[:, peer, :, lanes], dst_ref=out_ref.at[i, :, :, lanes],
                send_sem=bulk_send.at[piece, o], recv_sem=bulk_recv.at[piece, o],
                device_id={"rows": peer},
            )
            copy.start()
            bulk.append(copy)

    for load in loads[:5]:
        load.wait()
    row_data = jnp.concatenate(
        [r[...].astype(F32) for r in (node_ref, fold_ref, grad_ref, hess_ref)], 0
    )
    dense = dense_ref[...].astype(F32)
    for p in range(NR):
        small[p] = jnp.concatenate(
            [row_data, dense[p * PER : (p + 1) * PER], jnp.zeros((12 - PER, 128), F32)], 0
        ).astype(BF16)

    loads[5].wait()
    for piece in range(EARLY):
        turn_piece(piece)
    pl.semaphore_wait(barrier, NR - 1 + NB - 1)

    copies = []
    for o in range(1, NR):
        peer = lax.rem(i + o, NR)
        copy = pltpu.make_async_remote_copy(
            src_ref=small.at[peer], dst_ref=gathered.at[i],
            send_sem=small_send.at[o], recv_sem=small_recv.at[o], device_id={"rows": peer},
        )
        copy.start()
        copies.append(copy)
    own_small = pltpu.make_async_copy(small.at[i], gathered.at[i], local_sem.at[0])
    own_small.start()

    bulk = []
    for piece in range(EARLY):
        send_piece(piece)
    own_small.wait()
    for copy in copies:
        copy.wait()
    tiles = [gathered[p].astype(F32) for p in range(NR)]
    lines = [jnp.concatenate([t[n : n + 1] for t in tiles], 0) for n in range(4 + PER)]
    kinds[0] = jnp.concatenate(lines[0:2], 0).astype(BF16)
    kinds[1] = jnp.concatenate(lines[2:4], 0).astype(BF16)
    for n in range(PER):
        kinds[2 + n] = jnp.concatenate([lines[4 + n]] * 2, 0).astype(BF16)
    metas = []
    for o in range(1, NB):
        peer = lax.rem(b + o, NB)
        copy = pltpu.make_async_remote_copy(
            src_ref=kinds.at[0:2], dst_ref=meta_ref.at[b, 0:2],
            send_sem=meta_send.at[o], recv_sem=meta_recv.at[o], device_id={"bundles": peer},
        )
        copy.start()
        metas.append(copy)
        copy = pltpu.make_async_remote_copy(
            src_ref=kinds.at[2 + jnp.minimum(peer, PER - 1)], dst_ref=meta_ref.at[b, 2],
            send_sem=dense_send.at[o], recv_sem=dense_recv.at[o], device_id={"bundles": peer},
        )
        copy.start()
        metas.append(copy)
    own_meta = pltpu.make_async_copy(kinds.at[0:2], meta_ref.at[b, 0:2], local_sem.at[2])
    own_meta.start()
    own_dense = pltpu.make_async_copy(
        kinds.at[2 + jnp.minimum(b, PER - 1)], meta_ref.at[b, 2], local_sem.at[3]
    )
    own_dense.start()
    for piece in range(EARLY, PIECES):
        turn_piece(piece)
        send_piece(piece)
    own_bulk = pltpu.make_async_copy(level.at[:, i], out_ref.at[i], local_sem.at[1])
    own_bulk.start()
    own_meta.wait()
    own_dense.wait()
    for copy in metas:
        copy.wait()

    code = lax.broadcasted_iota(jnp.int32, (32, 128), 0)
    node_of = jnp.where(code < PAIRS, code % NODES, -1).astype(F32)
    fold_of = (code // NODES).astype(F32)
    rows = bins_ref.shape[0]

    def weights_out(p):
        lanes = pl.ds(pl.multiple_of(p * rows, rows), rows)
        return pltpu.make_async_copy(weight.at[:, lanes], weight_out.at[:, lanes], weight_sem.at[p])

    for n in range(NB):
        rows_of[n] = meta_ref[n].astype(F32)

    def prepare(p, most):
        first = pl.multiple_of(p * rows, rows)
        for n in range(0, NB, 2):
            above = below = size = 0.0
            for m in (n, n + 1):
                lanes = pl.ds(pl.multiple_of(first + m * 128, 128), 128)
                node, fold, grad, hess = (
                    jnp.broadcast_to(rows_of[m, kind, pl.ds(p + line, 1), :], (32, 128))
                    for kind, line in ((0, 0), (0, NR), (1, 0), (1, NR))
                )
                here = node == node_of
                grad = jnp.where(here & (fold != fold_of), grad, 0.0)
                hess = jnp.where(here & (fold == fold_of), hess, 0.0)
                weight[0:32, lanes] = grad.astype(F8)
                weight[32:64, lanes] = hess.astype(F8)
                above = above + jnp.maximum(grad, 0.0)
                below = below - jnp.minimum(grad, 0.0)
                size = size + hess
                dense_row[:, lanes] = rows_of[m, 2, pl.ds(p, 1), :]
            for sizes in (above, below, size):
                most = jnp.maximum(most, jnp.sum(sizes, 1, keepdims=True))
        weights_out(p).start()
        return most

    most = lax.fori_loop(0, NR, prepare, jnp.zeros((32, 1), F32))
    most_ref[...] = jnp.broadcast_to(most, (32, 128))
    own_most = pltpu.make_async_copy(most_ref, most_out, local_sem.at[4])
    own_most.start()
    own_best = pltpu.make_async_copy(dense_row, dense_out, local_sem.at[5])
    own_best.start()
    own_bulk.wait()
    own_most.wait()
    for p in range(NR):
        weights_out(p).wait()
    for copy in bulk:
        copy.wait()
    own_best.wait()


def exchange(bundle_bins, block_mask, dense_bins, row_data):
    anywhere = pl.BlockSpec(memory_space=pl.ANY)
    rows = bundle_bins.shape[0]
    dma = pltpu.SemaphoreType.DMA
    return pl.pallas_call(
        exchange_kernel,
        out_shape=(
            jax.ShapeDtypeStruct((NR, 2, 16, rows), BF16),
            jax.ShapeDtypeStruct((64, NR * rows), F8),
            jax.ShapeDtypeStruct((32, 128), F32),
            jax.ShapeDtypeStruct((1, NR * rows), F32),
        ),
        in_specs=[anywhere] * 7,
        out_specs=(anywhere,) * 4,
        scratch_shapes=[
            *(pltpu.VMEM(v.shape, v.dtype) for v in (bundle_bins, block_mask, dense_bins, *row_data)),
            dma((6 + PIECES,)),
            pltpu.VMEM((2, NR, 16, rows), BF16),
            pltpu.VMEM((NR, 16, 128), BF16),
            pltpu.VMEM((NR, 16, 128), BF16),
            pltpu.VMEM((2 + PER, 16, 128), BF16),
            pltpu.VMEM((NB, 3, 16, 128), BF16),
            pltpu.VMEM((NB, 3, 16, 128), F32),
            pltpu.VMEM((64, NR * rows), F8),
            pltpu.VMEM((32, 128), F32),
            pltpu.VMEM((1, NR * rows), F32),
            dma((6,)), dma((NR,)),
            dma((NR,)), dma((NR,)), dma((PIECES, NR)), dma((PIECES, NR)),
            dma((NB,)), dma((NB,)), dma((NB,)), dma((NB,)),
        ],
        compiler_params=pltpu.CompilerParams(
            collective_id=0, has_side_effects=True, vmem_limit_bytes=VMEM_BYTES
        ),
        name="exchange",
    )(bundle_bins, block_mask, dense_bins, *row_data)


def finish_kernel(
    narrow, level_hbm, weight_hbm, dense_hbm, rows_all, dense_all,
    level_ref, weight, dense_row, lev, hist, best, dense_best, dense_own,
    sems, send_a, recv_a, send_b, recv_b, send_c, recv_c,
):
    i = lax.axis_index("rows")
    b = lax.axis_index("bundles")
    rows = level_ref.shape[3]
    total = NR * rows
    chunk = 1024
    dtype = F8 if narrow else BF16
    loads = [
        pltpu.make_async_copy(source, target, sems.at[n])
        for n, (source, target) in enumerate(
            ((level_hbm, level_ref), (weight_hbm, weight), (dense_hbm, dense_row))
        )
    ]
    for load in loads:
        load.start()
    barrier = pltpu.get_barrier_semaphore()
    for o in range(1, NR):
        pl.semaphore_signal(barrier, inc=1, device_id={"rows": lax.rem(i + o, NR)})
    for o in range(1, NB):
        pl.semaphore_signal(barrier, inc=1, device_id={"bundles": lax.rem(b + o, NB)})

    loads[0].wait()

    def spread(p, _):
        first = pl.multiple_of(p * rows, rows)
        lev[0:16, pl.ds(first, rows)] = level_ref[p, 0].astype(F32)
        lev[16:32, pl.ds(first, rows)] = level_ref[p, 1].astype(F32)
        return 0

    lax.fori_loop(0, NR, spread, 0)
    loads[1].wait()
    loads[2].wait()
    def feature(source, j):
        acc = None
        for k in range(0, total, chunk):
            w = weight[:, k : k + chunk].astype(dtype)
            part = sums_of(source[pl.ds(j, 1), k : k + chunk].astype(BF16), w, dtype)
            acc = part if acc is None else acc + part
        return acc

    def across(source, peer):
        return pltpu.make_async_remote_copy(
            src_ref=dense_best, dst_ref=dense_own.at[source],
            send_sem=send_a.at[peer], recv_sem=recv_a.at[source], device_id={"bundles": peer},
        )

    def own_across(source):
        return pltpu.make_async_copy(dense_best, dense_own.at[source], sems.at[3])

    def along(o, source, target, send, recv):
        return pltpu.make_async_remote_copy(
            src_ref=source, dst_ref=target.at[i],
            send_sem=send.at[o], recv_sem=recv.at[o], device_id={"rows": lax.rem(i + o, NR)},
        )

    hist[...] = jnp.zeros_like(hist)
    dense = feature(dense_row, 0)
    dense_best[...] = jnp.broadcast_to(best_of(dense, dense), (8, 128))

    def pair(p, _):
        @pl.when(p == 1)
        def _():
            pl.semaphore_wait(barrier, NR - 1 + NB - 1)
            for source in range(PER):
                @pl.when(b == source)
                def _():
                    for peer in range(NB):
                        if peer != source:
                            across(source, peer).start()
                    own_across(source).start()

        @pl.when(p == 10)
        def _():
            for source in range(PER):
                @pl.when(b == source)
                def _():
                    own_across(source).wait()
                    for peer in range(NB):
                        if peer != source:
                            across(source, peer).wait_send()

                @pl.when(b != source)
                def _():
                    across(source, 0).wait_recv()
            for o in range(1, NR):
                along(o, dense_own, dense_all, send_c, recv_c).start()
            pltpu.make_async_copy(dense_own, dense_all.at[i], sems.at[4]).start()

        best[pl.ds(jnp.maximum(p - 1, 0), 1), :] = best_of(hist[0], hist[1])
        first = feature(lev, p)
        second = feature(lev, p + 16)
        hist[0] = first
        hist[1] = second
        return 0

    lax.fori_loop(0, 16, pair, 0)
    best[15:16, :] = best_of(hist[0], hist[1])

    pltpu.make_async_copy(dense_own, dense_all.at[i], sems.at[4]).wait()
    for o in range(1, NR):
        along(o, dense_own, dense_all, send_c, recv_c).wait()
    for o in range(1, NR):
        along(o, best, rows_all, send_b, recv_b).start()
    own = pltpu.make_async_copy(best, rows_all.at[i], sems.at[5])
    own.start()
    own.wait()
    for o in range(1, NR):
        along(o, best, rows_all, send_b, recv_b).wait()


def finish(narrow, level, weight, dense):
    anywhere = pl.BlockSpec(memory_space=pl.ANY)
    dma = pltpu.SemaphoreType.DMA
    return pl.pallas_call(
        functools.partial(finish_kernel, narrow),
        out_shape=(
            jax.ShapeDtypeStruct((NR, 16, 128), F32),
            jax.ShapeDtypeStruct((NR, PER, 8, 128), F32),
        ),
        in_specs=[anywhere] * 3,
        out_specs=(anywhere, anywhere),
        scratch_shapes=[
            pltpu.VMEM(level.shape, BF16),
            pltpu.VMEM(weight.shape, F8),
            pltpu.VMEM(dense.shape, F32),
            pltpu.VMEM((32, weight.shape[1]), F32),
            pltpu.VMEM((2, 128, 128), F32),
            pltpu.VMEM((16, 128), F32),
            pltpu.VMEM((8, 128), F32),
            pltpu.VMEM((PER, 8, 128), F32),
            dma((6,)), dma((NB,)), dma((PER,)), dma((NR,)), dma((NR,)), dma((NR,)), dma((NR,)),
        ],
        compiler_params=pltpu.CompilerParams(
            collective_id=1 if narrow else 2, has_side_effects=True, vmem_limit_bytes=VMEM_BYTES
        ),
        name="finish8" if narrow else "finish16",
    )(level, weight, dense)


def assemble_kernel(rows_ref, dense_ref, bundle_out, dense_out):
    turned = rows_ref[...].reshape(NR * 16, 128).T
    pieces = [dense_ref[r, d, 0:1, :] for r in range(NR) for d in range(PER)]
    dense = jnp.concatenate(pieces + [jnp.zeros((128 - DENSE, 128), F32)], 0).T
    for k in range(FOLDS):
        nodes = slice(k * NODES, (k + 1) * NODES)
        bundle_out[k, :, 0:128] = turned[nodes]
        bundle_out[k, :, 128:256] = turned[32:64][nodes]
        dense_out[k] = dense[nodes, 0:DENSE]


def assemble(rows_all, dense_all):
    return pl.pallas_call(
        assemble_kernel,
        out_shape=(
            jax.ShapeDtypeStruct((FOLDS, NODES, 256), F32),
            jax.ShapeDtypeStruct((FOLDS, NODES, DENSE), F32),
        ),
        name="assemble",
    )(rows_all, dense_all)


def local(dense_bins, bundle_bins, block_mask, node_ids, fold_ids, grads, hessians):
    row_data = [v.reshape(1, -1) for v in (node_ids, fold_ids, grads, hessians)]
    level, weight, most, dense = exchange(bundle_bins, block_mask, dense_bins, row_data)
    rows_all, dense_all = lax.cond(
        jnp.max(most) <= EXACT,
        functools.partial(finish, True), functools.partial(finish, False),
        level, weight, dense,
    )
    return assemble(rows_all, dense_all)


def solution(mesh):
    placed = (
        P(None, ("rows", "bundles")),
        P("rows", "bundles"),
        P("rows", "bundles"),
        P(("rows", "bundles")),
        P(("rows", "bundles")),
        P(("rows", "bundles")),
        P(("rows", "bundles")),
    )
    return jax.shard_map(
        local,
        mesh=mesh,
        in_specs=placed,
        out_specs=(P(None, None, "bundles"), P()),
        check_vma=False,
    )
```

```python
import functools

import jax
import jax.numpy as jnp
from jax import lax
from jax.experimental import pallas as pl
from jax.experimental.pallas import tpu as pltpu
from jax.sharding import PartitionSpec as P

NODES = 5
FOLDS = 5
PAIRS = FOLDS * NODES
NR = 8
NB = 16
DENSE = 40
PER = DENSE // NR
PIECES = 2
EARLY = 1
F32 = jnp.float32
BF16 = jnp.bfloat16
F8 = jnp.float8_e4m3fn
EXACT = 512.0
VMEM_BYTES = 67043328


def lanes_of():
    return lax.broadcasted_iota(jnp.int32, (128, 128), 1)


def prefix(half):
    base = jnp.broadcast_to(pltpu.roll(half[127:128], 64, 1), (128, 128))
    return half + jnp.where(lanes_of() >= 64, base, 0.0)


def total_of(left):
    top = left[127:128]
    return jnp.where(lanes_of()[0:1] >= 64, top, pltpu.roll(top, 64, 1))


def train_of(left):
    def from_right(v, n):
        return pltpu.roll(v, 128 - n, 1)

    folds = left + from_right(left, 5)
    folds = folds + from_right(folds, 10) + from_right(left, 20)
    folds = jnp.where(lanes_of() % 32 < NODES, folds, 0.0)
    spread = folds + pltpu.roll(folds, 5, 1)
    spread = spread + pltpu.roll(spread, 10, 1) + pltpu.roll(folds, 20, 1)
    return spread - left


def best_of(first, second):
    lane = lanes_of()
    last = (lax.broadcasted_iota(jnp.int32, (128, 128), 0) == 127) & (lane >= 64)
    even = lane % 64 < 32
    first, second = prefix(first), prefix(second)
    grad = jnp.where(even, first, pltpu.roll(second, 32, 1))
    hess = train_of(jnp.where(even, pltpu.roll(first, 96, 1), second))
    rest = total_of(grad) - grad
    gain = grad * grad / (hess + 1.0) + rest * rest / (total_of(hess) - hess + 1.0)
    best = jnp.max(jnp.where(last, -1.0, gain), 0, keepdims=True)
    return jnp.maximum(best, pltpu.roll(best, 64, 1))


def sums_of(row, w, dtype):
    rows = row.shape[1]
    high = jnp.where(row >= 128, jnp.ones((), BF16), jnp.zeros((), BF16))
    low = jnp.broadcast_to(row - high * BF16(128), (128, rows))
    bins = lax.broadcasted_iota(jnp.int32, (128, rows), 0).astype(BF16)
    step = jnp.where(low <= bins, jnp.ones((128, rows), dtype), jnp.zeros((128, rows), dtype))
    side = jnp.broadcast_to(high, (64, rows))
    zero = jnp.zeros((64, rows), dtype)
    right = jnp.concatenate([jnp.where(side == 0, w, zero), jnp.where(side != 0, w, zero)], 0)
    return lax.dot_general(step, right, (((1,), (1,)), ((), ())), preferred_element_type=F32)


def exchange_kernel(
    bins_hbm, mask_hbm, dense_hbm, node_hbm, fold_hbm, grad_hbm, hess_hbm,
    out_ref, weight_out, most_out, dense_out,
    bins_ref, mask_ref, dense_ref, node_ref, fold_ref, grad_ref, hess_ref, input_sem,
    level, small, gathered, kinds, meta_ref, rows_of, weight, most_ref, dense_row,
    local_sem, weight_sem, small_send, small_recv, bulk_send, bulk_recv, meta_send, meta_recv, dense_send, dense_recv,
):
    i = lax.axis_index("rows")
    b = lax.axis_index("bundles")
    barrier = pltpu.get_barrier_semaphore()
    for o in range(1, NR):
        pl.semaphore_signal(barrier, inc=1, device_id={"rows": lax.rem(i + o, NR)})
    for o in range(1, NB):
        pl.semaphore_signal(barrier, inc=1, device_id={"bundles": lax.rem(b + o, NB)})
    loads = [
        pltpu.make_async_copy(source, target, input_sem.at[n])
        for n, (source, target) in enumerate(
            (
                (node_hbm, node_ref), (fold_hbm, fold_ref), (grad_hbm, grad_ref), (hess_hbm, hess_ref),
                (dense_hbm, dense_ref), (mask_hbm, mask_ref),
            )
        )
    ]
    piece_rows = bins_ref.shape[0] // PIECES
    bins_loads = [
        pltpu.make_async_copy(
            bins_hbm.at[pl.ds(n * piece_rows, piece_rows)],
            bins_ref.at[pl.ds(n * piece_rows, piece_rows)],
            input_sem.at[6 + n],
        )
        for n in range(PIECES)
    ]
    for load in loads + bins_loads:
        load.start()

    def turn_piece(piece):
        bins_loads[piece].wait()

        def block(t, _):
            rows = pl.ds(pl.multiple_of(t * 128, 128), 128)
            marks = mask_ref[pl.ds(t, 1), :]
            values = jnp.where(marks > 0, bins_ref[rows, :], 0).astype(F32)
            turned = values.T.astype(BF16)
            for s in range(2):
                for p in range(NR):
                    first = s * 128 + p * 16
                    level[s, p, :, rows] = turned[first : first + 16]
            return 0

        blocks = piece_rows // 128
        lax.fori_loop(piece * blocks, (piece + 1) * blocks, block, 0)

    def send_piece(piece):
        lanes = pl.ds(piece * piece_rows, piece_rows)
        for o in range(1, NR):
            peer = lax.rem(i + o, NR)
            copy = pltpu.make_async_remote_copy(
                src_ref=level.at[:, peer, :, lanes], dst_ref=out_ref.at[i, :, :, lanes],
                send_sem=bulk_send.at[piece, o], recv_sem=bulk_recv.at[piece, o],
                device_id={"rows": peer},
            )
            copy.start()
            bulk.append(copy)

    for load in loads[:5]:
        load.wait()
    row_data = jnp.concatenate(
        [r[...].astype(F32) for r in (node_ref, fold_ref, grad_ref, hess_ref)], 0
    )
    dense = dense_ref[...].astype(F32)
    for p in range(NR):
        small[p] = jnp.concatenate(
            [row_data, dense[p * PER : (p + 1) * PER], jnp.zeros((12 - PER, 128), F32)], 0
        ).astype(BF16)

    loads[5].wait()
    for piece in range(EARLY):
        turn_piece(piece)
    pl.semaphore_wait(barrier, NR - 1 + NB - 1)

    copies = []
    for o in range(1, NR):
        peer = lax.rem(i + o, NR)
        copy = pltpu.make_async_remote_copy(
            src_ref=small.at[peer], dst_ref=gathered.at[i],
            send_sem=small_send.at[o], recv_sem=small_recv.at[o], device_id={"rows": peer},
        )
        copy.start()
        copies.append(copy)
    own_small = pltpu.make_async_copy(small.at[i], gathered.at[i], local_sem.at[0])
    own_small.start()

    bulk = []
    for piece in range(EARLY):
        send_piece(piece)
    own_small.wait()
    for copy in copies:
        copy.wait()
    tiles = [gathered[p].astype(F32) for p in range(NR)]
    lines = [jnp.concatenate([t[n : n + 1] for t in tiles], 0) for n in range(4 + PER)]
    kinds[0] = jnp.concatenate(lines[0:2], 0).astype(BF16)
    kinds[1] = jnp.concatenate(lines[2:4], 0).astype(BF16)
    for n in range(PER):
        kinds[2 + n] = jnp.concatenate([lines[4 + n]] * 2, 0).astype(BF16)
    metas = []
    for o in range(1, NB):
        peer = lax.rem(b + o, NB)
        copy = pltpu.make_async_remote_copy(
            src_ref=kinds.at[0:2], dst_ref=meta_ref.at[b, 0:2],
            send_sem=meta_send.at[o], recv_sem=meta_recv.at[o], device_id={"bundles": peer},
        )
        copy.start()
        metas.append(copy)
        copy = pltpu.make_async_remote_copy(
            src_ref=kinds.at[2 + jnp.minimum(peer, PER - 1)], dst_ref=meta_ref.at[b, 2],
            send_sem=dense_send.at[o], recv_sem=dense_recv.at[o], device_id={"bundles": peer},
        )
        copy.start()
        metas.append(copy)
    own_meta = pltpu.make_async_copy(kinds.at[0:2], meta_ref.at[b, 0:2], local_sem.at[2])
    own_meta.start()
    own_dense = pltpu.make_async_copy(
        kinds.at[2 + jnp.minimum(b, PER - 1)], meta_ref.at[b, 2], local_sem.at[3]
    )
    own_dense.start()
    for piece in range(EARLY, PIECES):
        turn_piece(piece)
        send_piece(piece)
    own_bulk = pltpu.make_async_copy(level.at[:, i], out_ref.at[i], local_sem.at[1])
    own_bulk.start()
    own_meta.wait()
    own_dense.wait()
    for copy in metas:
        copy.wait()

    code = lax.broadcasted_iota(jnp.int32, (32, 128), 0)
    node_of = jnp.where(code < PAIRS, code % NODES, -1).astype(F32)
    fold_of = (code // NODES).astype(F32)
    rows = bins_ref.shape[0]

    def weights_out(p):
        lanes = pl.ds(pl.multiple_of(p * rows, rows), rows)
        return pltpu.make_async_copy(weight.at[:, lanes], weight_out.at[:, lanes], weight_sem.at[p])

    for n in range(NB):
        rows_of[n] = meta_ref[n].astype(F32)

    def prepare(p, most):
        first = pl.multiple_of(p * rows, rows)
        for n in range(0, NB, 2):
            above = below = size = 0.0
            for m in (n, n + 1):
                lanes = pl.ds(pl.multiple_of(first + m * 128, 128), 128)
                node, fold, grad, hess = (
                    jnp.broadcast_to(rows_of[m, kind, pl.ds(p + line, 1), :], (32, 128))
                    for kind, line in ((0, 0), (0, NR), (1, 0), (1, NR))
                )
                here = node == node_of
                grad = jnp.where(here & (fold != fold_of), grad, 0.0)
                hess = jnp.where(here & (fold == fold_of), hess, 0.0)
                weight[0:32, lanes] = grad.astype(F8)
                weight[32:64, lanes] = hess.astype(F8)
                above = above + jnp.maximum(grad, 0.0)
                below = below - jnp.minimum(grad, 0.0)
                size = size + hess
                dense_row[:, lanes] = rows_of[m, 2, pl.ds(p, 1), :]
            for sizes in (above, below, size):
                most = jnp.maximum(most, jnp.sum(sizes, 1, keepdims=True))
        weights_out(p).start()
        return most

    most = lax.fori_loop(0, NR, prepare, jnp.zeros((32, 1), F32))
    most_ref[...] = jnp.broadcast_to(jnp.max(most, 0, keepdims=True), (8, 128))
    own_most = pltpu.make_async_copy(most_ref, most_out, local_sem.at[4])
    own_most.start()
    own_best = pltpu.make_async_copy(dense_row, dense_out, local_sem.at[5])
    own_best.start()
    own_bulk.wait()
    own_most.wait()
    for p in range(NR):
        weights_out(p).wait()
    for copy in bulk:
        copy.wait()
    own_best.wait()


def exchange(bundle_bins, block_mask, dense_bins, row_data):
    anywhere = pl.BlockSpec(memory_space=pl.ANY)
    rows = bundle_bins.shape[0]
    dma = pltpu.SemaphoreType.DMA
    return pl.pallas_call(
        exchange_kernel,
        out_shape=(
            jax.ShapeDtypeStruct((NR, 2, 16, rows), BF16),
            jax.ShapeDtypeStruct((64, NR * rows), F8),
            jax.ShapeDtypeStruct((8, 128), F32),
            jax.ShapeDtypeStruct((1, NR * rows), F32),
        ),
        in_specs=[anywhere] * 7,
        out_specs=(anywhere,) * 4,
        scratch_shapes=[
            *(pltpu.VMEM(v.shape, v.dtype) for v in (bundle_bins, block_mask, dense_bins, *row_data)),
            dma((6 + PIECES,)),
            pltpu.VMEM((2, NR, 16, rows), BF16),
            pltpu.VMEM((NR, 16, 128), BF16),
            pltpu.VMEM((NR, 16, 128), BF16),
            pltpu.VMEM((2 + PER, 16, 128), BF16),
            pltpu.VMEM((NB, 3, 16, 128), BF16),
            pltpu.VMEM((NB, 3, 16, 128), F32),
            pltpu.VMEM((64, NR * rows), F8),
            pltpu.VMEM((8, 128), F32),
            pltpu.VMEM((1, NR * rows), F32),
            dma((6,)), dma((NR,)),
            dma((NR,)), dma((NR,)), dma((PIECES, NR)), dma((PIECES, NR)),
            dma((NB,)), dma((NB,)), dma((NB,)), dma((NB,)),
        ],
        compiler_params=pltpu.CompilerParams(
            collective_id=0, has_side_effects=True, vmem_limit_bytes=VMEM_BYTES
        ),
        name="exchange",
    )(bundle_bins, block_mask, dense_bins, *row_data)


def finish_kernel(
    narrow, level_hbm, weight_hbm, dense_hbm, rows_all, dense_all,
    level_ref, weight, dense_row, lev, hist, best, dense_best, dense_own,
    sems, send_a, recv_a, send_b, recv_b, send_c, recv_c,
):
    i = lax.axis_index("rows")
    b = lax.axis_index("bundles")
    rows = level_ref.shape[3]
    total = NR * rows
    chunk = 1024
    dtype = F8 if narrow else BF16
    loads = [
        pltpu.make_async_copy(source, target, sems.at[n])
        for n, (source, target) in enumerate(
            ((dense_hbm, dense_row), (weight_hbm, weight), (level_hbm, level_ref))
        )
    ]
    for load in loads:
        load.start()
    barrier = pltpu.get_barrier_semaphore()
    for o in range(1, NR):
        pl.semaphore_signal(barrier, inc=1, device_id={"rows": lax.rem(i + o, NR)})
    for o in range(1, NB):
        pl.semaphore_signal(barrier, inc=1, device_id={"bundles": lax.rem(b + o, NB)})

    def feature(source, j):
        acc = None
        for k in range(0, total, chunk):
            w = weight[:, k : k + chunk].astype(dtype)
            part = sums_of(source[pl.ds(j, 1), k : k + chunk].astype(BF16), w, dtype)
            acc = part if acc is None else acc + part
        return acc

    def across(source, peer):
        return pltpu.make_async_remote_copy(
            src_ref=dense_best, dst_ref=dense_own.at[source],
            send_sem=send_a.at[peer], recv_sem=recv_a.at[source], device_id={"bundles": peer},
        )

    def own_across(source):
        return pltpu.make_async_copy(dense_best, dense_own.at[source], sems.at[3])

    def along(o, source, target, send, recv):
        return pltpu.make_async_remote_copy(
            src_ref=source, dst_ref=target.at[i],
            send_sem=send.at[o], recv_sem=recv.at[o], device_id={"rows": lax.rem(i + o, NR)},
        )

    loads[0].wait()
    loads[1].wait()
    dense = feature(dense_row, 0)
    hist[0] = dense
    hist[1] = dense
    loads[2].wait()

    def spread(p, _):
        first = pl.multiple_of(p * rows, rows)
        lev[0:16, pl.ds(first, rows)] = level_ref[p, 0].astype(F32)
        lev[16:32, pl.ds(first, rows)] = level_ref[p, 1].astype(F32)
        return 0

    lax.fori_loop(0, NR, spread, 0)

    def pair(p, _):
        @pl.when(p == 1)
        def _():
            dense_best[...] = jnp.broadcast_to(best[15:16, :], (8, 128))

        @pl.when(p == 2)
        def _():
            pl.semaphore_wait(barrier, NR - 1 + NB - 1)
            for source in range(PER):
                @pl.when(b == source)
                def _():
                    for peer in range(NB):
                        if peer != source:
                            across(source, peer).start()
                    own_across(source).start()

        @pl.when(p == 10)
        def _():
            for source in range(PER):
                @pl.when(b == source)
                def _():
                    own_across(source).wait()
                    for peer in range(NB):
                        if peer != source:
                            across(source, peer).wait_send()

                @pl.when(b != source)
                def _():
                    across(source, 0).wait_recv()
            for o in range(1, NR):
                along(o, dense_own, dense_all, send_c, recv_c).start()
            pltpu.make_async_copy(dense_own, dense_all.at[i], sems.at[4]).start()

        best[pl.ds(lax.rem(p + 15, 16), 1), :] = best_of(hist[0], hist[1])
        first = feature(lev, p)
        second = feature(lev, p + 16)
        hist[0] = first
        hist[1] = second
        return 0

    lax.fori_loop(0, 16, pair, 0)
    best[15:16, :] = best_of(hist[0], hist[1])

    pltpu.make_async_copy(dense_own, dense_all.at[i], sems.at[4]).wait()
    for o in range(1, NR):
        along(o, dense_own, dense_all, send_c, recv_c).wait()
    for o in range(1, NR):
        along(o, best, rows_all, send_b, recv_b).start()
    own = pltpu.make_async_copy(best, rows_all.at[i], sems.at[5])
    own.start()
    own.wait()
    for o in range(1, NR):
        along(o, best, rows_all, send_b, recv_b).wait()


def finish(narrow, level, weight, dense):
    anywhere = pl.BlockSpec(memory_space=pl.ANY)
    dma = pltpu.SemaphoreType.DMA
    return pl.pallas_call(
        functools.partial(finish_kernel, narrow),
        out_shape=(
            jax.ShapeDtypeStruct((NR, 16, 128), F32),
            jax.ShapeDtypeStruct((NR, PER, 8, 128), F32),
        ),
        in_specs=[anywhere] * 3,
        out_specs=(anywhere, anywhere),
        scratch_shapes=[
            pltpu.VMEM(level.shape, BF16),
            pltpu.VMEM(weight.shape, F8),
            pltpu.VMEM(dense.shape, F32),
            pltpu.VMEM((32, weight.shape[1]), F32),
            pltpu.VMEM((2, 128, 128), F32),
            pltpu.VMEM((16, 128), F32),
            pltpu.VMEM((8, 128), F32),
            pltpu.VMEM((PER, 8, 128), F32),
            dma((6,)), dma((NB,)), dma((PER,)), dma((NR,)), dma((NR,)), dma((NR,)), dma((NR,)),
        ],
        compiler_params=pltpu.CompilerParams(
            collective_id=1 if narrow else 2, has_side_effects=True, vmem_limit_bytes=VMEM_BYTES
        ),
        name="finish8" if narrow else "finish16",
    )(level, weight, dense)


def assemble_kernel(rows_ref, dense_ref, bundle_out, dense_out):
    turned = rows_ref[...].reshape(NR * 16, 128).T
    pieces = [dense_ref[r, d, 0:1, :] for r in range(NR) for d in range(PER)]
    dense = jnp.concatenate(pieces + [jnp.zeros((128 - DENSE, 128), F32)], 0).T
    for k in range(FOLDS):
        nodes = slice(k * NODES, (k + 1) * NODES)
        bundle_out[k, :, 0:128] = turned[nodes]
        bundle_out[k, :, 128:256] = turned[32:64][nodes]
        dense_out[k] = dense[nodes, 0:DENSE]


def assemble(rows_all, dense_all):
    return pl.pallas_call(
        assemble_kernel,
        out_shape=(
            jax.ShapeDtypeStruct((FOLDS, NODES, 256), F32),
            jax.ShapeDtypeStruct((FOLDS, NODES, DENSE), F32),
        ),
        name="assemble",
    )(rows_all, dense_all)


def local(dense_bins, bundle_bins, block_mask, node_ids, fold_ids, grads, hessians):
    row_data = [v.reshape(1, -1) for v in (node_ids, fold_ids, grads, hessians)]
    level, weight, most, dense = exchange(bundle_bins, block_mask, dense_bins, row_data)
    rows_all, dense_all = lax.cond(
        most[0, 0] <= EXACT,
        functools.partial(finish, True), functools.partial(finish, False),
        level, weight, dense,
    )
    return assemble(rows_all, dense_all)


def solution(mesh):
    placed = (
        P(None, ("rows", "bundles")),
        P("rows", "bundles"),
        P("rows", "bundles"),
        P(("rows", "bundles")),
        P(("rows", "bundles")),
        P(("rows", "bundles")),
        P(("rows", "bundles")),
    )
    return jax.shard_map(
        local,
        mesh=mesh,
        in_specs=placed,
        out_specs=(P(None, None, "bundles"), P()),
        check_vma=False,
    )
```

```python
import functools

import jax
import jax.numpy as jnp
from jax import lax
from jax.experimental import pallas as pl
from jax.experimental.pallas import tpu as pltpu
from jax.sharding import PartitionSpec as P

NODES = 5
FOLDS = 5
PAIRS = FOLDS * NODES
NR = 8
NB = 16
DENSE = 40
PER = DENSE // NR
PIECES = 2
F32 = jnp.float32
BF16 = jnp.bfloat16
F8 = jnp.float8_e4m3fn
EXACT = 512.0
VMEM_BYTES = 67043328


def lanes_of():
    return lax.broadcasted_iota(jnp.int32, (128, 128), 1)


def prefix(half):
    base = jnp.broadcast_to(pltpu.roll(half[127:128], 64, 1), (128, 128))
    return half + jnp.where(lanes_of() >= 64, base, 0.0)


def total_of(left):
    top = left[127:128]
    return jnp.where(lanes_of()[0:1] >= 64, top, pltpu.roll(top, 64, 1))


def train_of(left):
    def from_right(v, n):
        return pltpu.roll(v, 128 - n, 1)

    folds = left + from_right(left, 5)
    folds = folds + from_right(folds, 10) + from_right(left, 20)
    folds = jnp.where(lanes_of() % 32 < NODES, folds, 0.0)
    spread = folds + pltpu.roll(folds, 5, 1)
    spread = spread + pltpu.roll(spread, 10, 1) + pltpu.roll(folds, 20, 1)
    return spread - left


def best_of(first, second):
    lane = lanes_of()
    last = (lax.broadcasted_iota(jnp.int32, (128, 128), 0) == 127) & (lane >= 64)
    even = lane % 64 < 32
    first, second = prefix(first), prefix(second)
    grad = jnp.where(even, first, pltpu.roll(second, 32, 1))
    hess = train_of(jnp.where(even, pltpu.roll(first, 96, 1), second))
    rest = total_of(grad) - grad
    gain = grad * grad / (hess + 1.0) + rest * rest / (total_of(hess) - hess + 1.0)
    best = jnp.max(jnp.where(last, -1.0, gain), 0, keepdims=True)
    return jnp.maximum(best, pltpu.roll(best, 64, 1))


def sums_of(row, w, dtype):
    rows = row.shape[1]
    high = jnp.where(row >= 128, jnp.ones((), BF16), jnp.zeros((), BF16))
    low = jnp.broadcast_to(row - high * BF16(128), (128, rows))
    bins = lax.broadcasted_iota(jnp.int32, (128, rows), 0).astype(BF16)
    step = jnp.where(low <= bins, jnp.ones((128, rows), dtype), jnp.zeros((128, rows), dtype))
    side = jnp.broadcast_to(high, (64, rows))
    zero = jnp.zeros((64, rows), dtype)
    right = jnp.concatenate([jnp.where(side == 0, w, zero), jnp.where(side != 0, w, zero)], 0)
    return lax.dot_general(step, right, (((1,), (1,)), ((), ())), preferred_element_type=F32)


def exchange_kernel(
    bins_hbm, mask_hbm, dense_hbm, node_hbm, fold_hbm, grad_hbm, hess_hbm,
    out_ref, late_out, weight_out, most_out, dense_out,
    bins_ref, mask_ref, dense_ref, node_ref, fold_ref, grad_ref, hess_ref, input_sem,
    level, small, gathered, kinds, meta_ref, rows_of, weight, most_ref, dense_row,
    local_sem, weight_sem, small_send, small_recv, bulk_send, bulk_recv, meta_send, meta_recv, dense_send, dense_recv,
):
    i = lax.axis_index("rows")
    b = lax.axis_index("bundles")
    barrier = pltpu.get_barrier_semaphore()
    for o in range(1, NR):
        pl.semaphore_signal(barrier, inc=1, device_id={"rows": lax.rem(i + o, NR)})
    for o in range(1, NB):
        pl.semaphore_signal(barrier, inc=1, device_id={"bundles": lax.rem(b + o, NB)})
    loads = [
        pltpu.make_async_copy(source, target, input_sem.at[n])
        for n, (source, target) in enumerate(
            (
                (node_hbm, node_ref), (fold_hbm, fold_ref), (grad_hbm, grad_ref), (hess_hbm, hess_ref),
                (dense_hbm, dense_ref), (mask_hbm, mask_ref),
            )
        )
    ]
    piece_rows = bins_ref.shape[0] // PIECES
    bins_loads = [
        pltpu.make_async_copy(
            bins_hbm.at[pl.ds(n * piece_rows, piece_rows)],
            bins_ref.at[pl.ds(n * piece_rows, piece_rows)],
            input_sem.at[6 + n],
        )
        for n in range(PIECES)
    ]
    for load in loads + bins_loads:
        load.start()

    def turn_piece(piece):
        bins_loads[piece].wait()

        def block(t, _):
            rows = pl.ds(pl.multiple_of(t * 128, 128), 128)
            marks = mask_ref[pl.ds(t, 1), :]
            values = jnp.where(marks > 0, bins_ref[rows, :], 0).astype(F32)
            turned = values.T.astype(BF16)
            for s in range(2):
                for p in range(NR):
                    first = s * 128 + p * 16
                    level[s, p, :, rows] = turned[first : first + 16]
            return 0

        blocks = piece_rows // 128
        lax.fori_loop(piece * blocks, (piece + 1) * blocks, block, 0)

    early = pl.ds(0, piece_rows)

    def send_early():
        for o in range(1, NR):
            peer = lax.rem(i + o, NR)
            copy = pltpu.make_async_remote_copy(
                src_ref=level.at[:, peer, :, early], dst_ref=out_ref.at[i],
                send_sem=bulk_send.at[o], recv_sem=bulk_recv.at[o], device_id={"rows": peer},
            )
            copy.start()
            bulk.append(copy)

    for load in loads[:5]:
        load.wait()
    row_data = jnp.concatenate(
        [r[...].astype(F32) for r in (node_ref, fold_ref, grad_ref, hess_ref)], 0
    )
    dense = dense_ref[...].astype(F32)
    for p in range(NR):
        small[p] = jnp.concatenate(
            [row_data, dense[p * PER : (p + 1) * PER], jnp.zeros((12 - PER, 128), F32)], 0
        ).astype(BF16)

    loads[5].wait()
    turn_piece(0)
    pl.semaphore_wait(barrier, NR - 1 + NB - 1)

    copies = []
    for o in range(1, NR):
        peer = lax.rem(i + o, NR)
        copy = pltpu.make_async_remote_copy(
            src_ref=small.at[peer], dst_ref=gathered.at[i],
            send_sem=small_send.at[o], recv_sem=small_recv.at[o], device_id={"rows": peer},
        )
        copy.start()
        copies.append(copy)
    own_small = pltpu.make_async_copy(small.at[i], gathered.at[i], local_sem.at[0])
    own_small.start()

    bulk = []
    send_early()
    own_small.wait()
    for copy in copies:
        copy.wait()
    tiles = [gathered[p].astype(F32) for p in range(NR)]
    lines = [jnp.concatenate([t[n : n + 1] for t in tiles], 0) for n in range(4 + PER)]
    kinds[0] = jnp.concatenate(lines[0:2], 0).astype(BF16)
    kinds[1] = jnp.concatenate(lines[2:4], 0).astype(BF16)
    for n in range(PER):
        kinds[2 + n] = jnp.concatenate([lines[4 + n]] * 2, 0).astype(BF16)
    metas = []
    for o in range(1, NB):
        peer = lax.rem(b + o, NB)
        copy = pltpu.make_async_remote_copy(
            src_ref=kinds.at[0:2], dst_ref=meta_ref.at[b, 0:2],
            send_sem=meta_send.at[o], recv_sem=meta_recv.at[o], device_id={"bundles": peer},
        )
        copy.start()
        metas.append(copy)
        copy = pltpu.make_async_remote_copy(
            src_ref=kinds.at[2 + jnp.minimum(peer, PER - 1)], dst_ref=meta_ref.at[b, 2],
            send_sem=dense_send.at[o], recv_sem=dense_recv.at[o], device_id={"bundles": peer},
        )
        copy.start()
        metas.append(copy)
    own_meta = pltpu.make_async_copy(kinds.at[0:2], meta_ref.at[b, 0:2], local_sem.at[2])
    own_meta.start()
    own_dense = pltpu.make_async_copy(
        kinds.at[2 + jnp.minimum(b, PER - 1)], meta_ref.at[b, 2], local_sem.at[3]
    )
    own_dense.start()
    own_bulk = pltpu.make_async_copy(level.at[:, i, :, early], out_ref.at[i], local_sem.at[1])
    own_bulk.start()
    turn_piece(1)
    late_copy = pltpu.make_async_copy(
        level.at[:, :, :, pl.ds(piece_rows, piece_rows)], late_out, local_sem.at[6]
    )
    late_copy.start()
    own_meta.wait()
    own_dense.wait()
    for copy in metas:
        copy.wait()

    code = lax.broadcasted_iota(jnp.int32, (32, 128), 0)
    node_of = jnp.where(code < PAIRS, code % NODES, -1).astype(F32)
    fold_of = (code // NODES).astype(F32)
    rows = bins_ref.shape[0]

    def weights_out(p):
        lanes = pl.ds(pl.multiple_of(p * rows, rows), rows)
        return pltpu.make_async_copy(weight.at[:, lanes], weight_out.at[:, lanes], weight_sem.at[p])

    for n in range(NB):
        rows_of[n] = meta_ref[n].astype(F32)

    def prepare(p, most):
        first = pl.multiple_of(p * rows, rows)
        for n in range(0, NB, 2):
            above = below = size = 0.0
            for m in (n, n + 1):
                lanes = pl.ds(pl.multiple_of(first + m * 128, 128), 128)
                node, fold, grad, hess = (
                    jnp.broadcast_to(rows_of[m, kind, pl.ds(p + line, 1), :], (32, 128))
                    for kind, line in ((0, 0), (0, NR), (1, 0), (1, NR))
                )
                here = node == node_of
                grad = jnp.where(here & (fold != fold_of), grad, 0.0)
                hess = jnp.where(here & (fold == fold_of), hess, 0.0)
                weight[0:32, lanes] = grad.astype(F8)
                weight[32:64, lanes] = hess.astype(F8)
                above = above + jnp.maximum(grad, 0.0)
                below = below - jnp.minimum(grad, 0.0)
                size = size + hess
                dense_row[:, lanes] = rows_of[m, 2, pl.ds(p, 1), :]
            for sizes in (above, below, size):
                most = jnp.maximum(most, jnp.sum(sizes, 1, keepdims=True))
        weights_out(p).start()
        return most

    most = lax.fori_loop(0, NR, prepare, jnp.zeros((32, 1), F32))
    most_ref[...] = jnp.broadcast_to(jnp.max(most, 0, keepdims=True), (8, 128))
    own_most = pltpu.make_async_copy(most_ref, most_out, local_sem.at[4])
    own_most.start()
    own_best = pltpu.make_async_copy(dense_row, dense_out, local_sem.at[5])
    own_best.start()
    own_bulk.wait()
    late_copy.wait()
    own_most.wait()
    for p in range(NR):
        weights_out(p).wait()
    for copy in bulk:
        copy.wait()
    own_best.wait()


def exchange(bundle_bins, block_mask, dense_bins, row_data):
    anywhere = pl.BlockSpec(memory_space=pl.ANY)
    rows = bundle_bins.shape[0]
    dma = pltpu.SemaphoreType.DMA
    return pl.pallas_call(
        exchange_kernel,
        out_shape=(
            jax.ShapeDtypeStruct((NR, 2, 16, rows // 2), BF16),
            jax.ShapeDtypeStruct((2, NR, 16, rows // 2), BF16),
            jax.ShapeDtypeStruct((64, NR * rows), F8),
            jax.ShapeDtypeStruct((8, 128), F32),
            jax.ShapeDtypeStruct((1, NR * rows), F32),
        ),
        in_specs=[anywhere] * 7,
        out_specs=(anywhere,) * 5,
        scratch_shapes=[
            *(pltpu.VMEM(v.shape, v.dtype) for v in (bundle_bins, block_mask, dense_bins, *row_data)),
            dma((6 + PIECES,)),
            pltpu.VMEM((2, NR, 16, rows), BF16),
            pltpu.VMEM((NR, 16, 128), BF16),
            pltpu.VMEM((NR, 16, 128), BF16),
            pltpu.VMEM((2 + PER, 16, 128), BF16),
            pltpu.VMEM((NB, 3, 16, 128), BF16),
            pltpu.VMEM((NB, 3, 16, 128), F32),
            pltpu.VMEM((64, NR * rows), F8),
            pltpu.VMEM((8, 128), F32),
            pltpu.VMEM((1, NR * rows), F32),
            dma((7,)), dma((NR,)),
            dma((NR,)), dma((NR,)), dma((NR,)), dma((NR,)),
            dma((NB,)), dma((NB,)), dma((NB,)), dma((NB,)),
        ],
        compiler_params=pltpu.CompilerParams(
            collective_id=0, has_side_effects=True, vmem_limit_bytes=VMEM_BYTES
        ),
        name="exchange",
    )(bundle_bins, block_mask, dense_bins, *row_data)


def finish_kernel(
    narrow, level_hbm, late_hbm, weight_hbm, dense_hbm, rows_all, dense_all,
    level_ref, late_ref, weight, dense_row, lev, hist, added, best, dense_best, dense_own,
    sems, send_a, recv_a, send_b, recv_b, send_c, recv_c, send_d, recv_d,
):
    i = lax.axis_index("rows")
    b = lax.axis_index("bundles")
    half = level_ref.shape[3]
    total = NR * 2 * half
    chunk = 1024
    dtype = F8 if narrow else BF16
    loads = [
        pltpu.make_async_copy(source, target, sems.at[n])
        for n, (source, target) in enumerate(
            ((dense_hbm, dense_row), (weight_hbm, weight), (level_hbm, level_ref))
        )
    ]
    for load in loads:
        load.start()
    barrier = pltpu.get_barrier_semaphore()
    for o in range(1, NR):
        pl.semaphore_signal(barrier, inc=1, device_id={"rows": lax.rem(i + o, NR)})
    for o in range(1, NB):
        pl.semaphore_signal(barrier, inc=1, device_id={"bundles": lax.rem(b + o, NB)})

    def feature(source, j, starts):
        acc = None
        for start in starts:
            for k in range(start, start + half, chunk):
                w = weight[:, k : k + chunk].astype(dtype)
                part = sums_of(source[pl.ds(j, 1), k : k + chunk].astype(BF16), w, dtype)
                acc = part if acc is None else acc + part
        return acc

    early_starts = range(0, total, 2 * half)
    late_starts = range(half, total, 2 * half)

    def across(source, peer):
        return pltpu.make_async_remote_copy(
            src_ref=dense_best, dst_ref=dense_own.at[source],
            send_sem=send_a.at[peer], recv_sem=recv_a.at[source], device_id={"bundles": peer},
        )

    def own_across(source):
        return pltpu.make_async_copy(dense_best, dense_own.at[source], sems.at[3])

    def along(o, source, target, send, recv):
        return pltpu.make_async_remote_copy(
            src_ref=source, dst_ref=target.at[i],
            send_sem=send.at[o], recv_sem=recv.at[o], device_id={"rows": lax.rem(i + o, NR)},
        )

    def late(o):
        peer = lax.rem(i + o, NR)
        return pltpu.make_async_remote_copy(
            src_ref=late_hbm.at[:, peer], dst_ref=late_ref.at[i],
            send_sem=send_d.at[o], recv_sem=recv_d.at[o], device_id={"rows": peer},
        )

    own_late = pltpu.make_async_copy(late_hbm.at[:, i], late_ref.at[i], sems.at[6])
    own_late.start()

    def spread_from(ref, offset):
        def spread(p, _):
            lanes = pl.ds(pl.multiple_of(p * (2 * half) + offset, half), half)
            lev[0:16, lanes] = ref[p, 0].astype(F32)
            lev[16:32, lanes] = ref[p, 1].astype(F32)
            return 0

        lax.fori_loop(0, NR, spread, 0)

    loads[0].wait()
    loads[1].wait()
    hist[32] = feature(dense_row, 0, range(0, total, half))
    loads[2].wait()
    spread_from(level_ref, 0)

    def first_half(q, _):
        @pl.when(q == 1)
        def _():
            pl.semaphore_wait(barrier, NR - 1 + NB - 1)
            for o in range(1, NR):
                late(o).start()
            dense_best[...] = jnp.broadcast_to(best[15:16, :], (8, 128))

        @pl.when(q == 2)
        def _():
            for source in range(PER):
                @pl.when(b == source)
                def _():
                    for peer in range(NB):
                        if peer != source:
                            across(source, peer).start()
                    own_across(source).start()

        best[15:16, :] = best_of(hist[32], hist[32])
        sums = [feature(lev, q + 8 * n, early_starts) for n in range(4)]
        for n in range(4):
            hist[q + 8 * n] = sums[n]
        return 0

    lax.fori_loop(0, 8, first_half, 0)
    own_late.wait()
    for o in range(1, NR):
        late(o).wait()
    spread_from(late_ref, half)

    def gains_of(q):
        sums = [hist[q + 8 * n] + added[n] for n in range(4)]
        best[pl.ds(q, 1), :] = best_of(sums[0], sums[2])
        best[pl.ds(q + 8, 1), :] = best_of(sums[1], sums[3])

    added[...] = jnp.zeros_like(added)

    def second_half(q, _):
        @pl.when(q == 2)
        def _():
            for source in range(PER):
                @pl.when(b == source)
                def _():
                    own_across(source).wait()
                    for peer in range(NB):
                        if peer != source:
                            across(source, peer).wait_send()

                @pl.when(b != source)
                def _():
                    across(source, 0).wait_recv()
            for o in range(1, NR):
                along(o, dense_own, dense_all, send_c, recv_c).start()
            pltpu.make_async_copy(dense_own, dense_all.at[i], sems.at[4]).start()

        old = jnp.maximum(q - 1, 0)
        gains_of(old)
        sums = [feature(lev, q + 8 * n, late_starts) for n in range(4)]
        for n in range(4):
            added[n] = sums[n]
        return 0

    lax.fori_loop(0, 8, second_half, 0)
    gains_of(7)

    pltpu.make_async_copy(dense_own, dense_all.at[i], sems.at[4]).wait()
    for o in range(1, NR):
        along(o, dense_own, dense_all, send_c, recv_c).wait()
    for o in range(1, NR):
        along(o, best, rows_all, send_b, recv_b).start()
    own = pltpu.make_async_copy(best, rows_all.at[i], sems.at[5])
    own.start()
    own.wait()
    for o in range(1, NR):
        along(o, best, rows_all, send_b, recv_b).wait()


def finish(narrow, level, late, weight, dense):
    anywhere = pl.BlockSpec(memory_space=pl.ANY)
    dma = pltpu.SemaphoreType.DMA
    return pl.pallas_call(
        functools.partial(finish_kernel, narrow),
        out_shape=(
            jax.ShapeDtypeStruct((NR, 16, 128), F32),
            jax.ShapeDtypeStruct((NR, PER, 8, 128), F32),
        ),
        in_specs=[anywhere] * 4,
        out_specs=(anywhere, anywhere),
        scratch_shapes=[
            pltpu.VMEM(level.shape, BF16),
            pltpu.VMEM(level.shape, BF16),
            pltpu.VMEM(weight.shape, F8),
            pltpu.VMEM(dense.shape, F32),
            pltpu.VMEM((32, weight.shape[1]), F32),
            pltpu.VMEM((33, 128, 128), F32),
            pltpu.VMEM((4, 128, 128), F32),
            pltpu.VMEM((16, 128), F32),
            pltpu.VMEM((8, 128), F32),
            pltpu.VMEM((PER, 8, 128), F32),
            dma((7,)), dma((NB,)), dma((PER,)), *(dma((NR,)) for _ in range(6)),
        ],
        compiler_params=pltpu.CompilerParams(
            collective_id=1 if narrow else 2, has_side_effects=True, vmem_limit_bytes=VMEM_BYTES
        ),
        name="finish8" if narrow else "finish16",
    )(level, late, weight, dense)


def assemble_kernel(rows_ref, dense_ref, bundle_out, dense_out):
    turned = rows_ref[...].reshape(NR * 16, 128).T
    pieces = [dense_ref[r, d, 0:1, :] for r in range(NR) for d in range(PER)]
    dense = jnp.concatenate(pieces + [jnp.zeros((128 - DENSE, 128), F32)], 0).T
    for k in range(FOLDS):
        nodes = slice(k * NODES, (k + 1) * NODES)
        bundle_out[k, :, 0:128] = turned[nodes]
        bundle_out[k, :, 128:256] = turned[32:64][nodes]
        dense_out[k] = dense[nodes, 0:DENSE]


def assemble(rows_all, dense_all):
    return pl.pallas_call(
        assemble_kernel,
        out_shape=(
            jax.ShapeDtypeStruct((FOLDS, NODES, 256), F32),
            jax.ShapeDtypeStruct((FOLDS, NODES, DENSE), F32),
        ),
        name="assemble",
    )(rows_all, dense_all)


def local(dense_bins, bundle_bins, block_mask, node_ids, fold_ids, grads, hessians):
    row_data = [v.reshape(1, -1) for v in (node_ids, fold_ids, grads, hessians)]
    level, late, weight, most, dense = exchange(bundle_bins, block_mask, dense_bins, row_data)
    rows_all, dense_all = lax.cond(
        most[0, 0] <= EXACT,
        functools.partial(finish, True), functools.partial(finish, False),
        level, late, weight, dense,
    )
    return assemble(rows_all, dense_all)


def solution(mesh):
    placed = (
        P(None, ("rows", "bundles")),
        P("rows", "bundles"),
        P("rows", "bundles"),
        P(("rows", "bundles")),
        P(("rows", "bundles")),
        P(("rows", "bundles")),
        P(("rows", "bundles")),
    )
    return jax.shard_map(
        local,
        mesh=mesh,
        in_specs=placed,
        out_specs=(P(None, None, "bundles"), P()),
        check_vma=False,
    )
```

```python
import functools

import jax
import jax.numpy as jnp
from jax import lax
from jax.experimental import pallas as pl
from jax.experimental.pallas import tpu as pltpu
from jax.sharding import PartitionSpec as P

NODES = 5
FOLDS = 5
PAIRS = FOLDS * NODES
NR = 8
NB = 16
DENSE = 40
PER = DENSE // NR
PIECES = 2
F32 = jnp.float32
BF16 = jnp.bfloat16
F8 = jnp.float8_e4m3fn
EXACT = 512.0
VMEM_BYTES = 67043328


def lanes_of():
    return lax.broadcasted_iota(jnp.int32, (128, 128), 1)


def prefix(half):
    base = jnp.broadcast_to(pltpu.roll(half[127:128], 64, 1), (128, 128))
    return half + jnp.where(lanes_of() >= 64, base, 0.0)


def total_of(left):
    top = left[127:128]
    return jnp.where(lanes_of()[0:1] >= 64, top, pltpu.roll(top, 64, 1))


def train_of(left):
    def from_right(v, n):
        return pltpu.roll(v, 128 - n, 1)

    folds = left + from_right(left, 5)
    folds = folds + from_right(folds, 10) + from_right(left, 20)
    folds = jnp.where(lanes_of() % 32 < NODES, folds, 0.0)
    spread = folds + pltpu.roll(folds, 5, 1)
    spread = spread + pltpu.roll(spread, 10, 1) + pltpu.roll(folds, 20, 1)
    return spread - left


def best_of(first, second):
    lane = lanes_of()
    last = (lax.broadcasted_iota(jnp.int32, (128, 128), 0) == 127) & (lane >= 64)
    even = lane % 64 < 32
    first, second = prefix(first), prefix(second)
    grad = jnp.where(even, first, pltpu.roll(second, 32, 1))
    hess = train_of(jnp.where(even, pltpu.roll(first, 96, 1), second))
    rest = total_of(grad) - grad
    gain = grad * grad / (hess + 1.0) + rest * rest / (total_of(hess) - hess + 1.0)
    best = jnp.max(jnp.where(last, -1.0, gain), 0, keepdims=True)
    return jnp.maximum(best, pltpu.roll(best, 64, 1))


def sums_of(row, w, dtype):
    rows = row.shape[1]
    high = jnp.where(row >= 128, jnp.ones((), BF16), jnp.zeros((), BF16))
    low = jnp.broadcast_to(row - high * BF16(128), (128, rows))
    bins = lax.broadcasted_iota(jnp.int32, (128, rows), 0).astype(BF16)
    step = jnp.where(low <= bins, jnp.ones((128, rows), dtype), jnp.zeros((128, rows), dtype))
    side = jnp.broadcast_to(high, (64, rows))
    zero = jnp.zeros((64, rows), dtype)
    right = jnp.concatenate([jnp.where(side == 0, w, zero), jnp.where(side != 0, w, zero)], 0)
    return lax.dot_general(step, right, (((1,), (1,)), ((), ())), preferred_element_type=F32)


def exchange_kernel(
    bins_hbm, mask_hbm, dense_hbm, node_hbm, fold_hbm, grad_hbm, hess_hbm,
    out_ref, late_out, weight_out, most_out, dense_out,
    bins_ref, mask_ref, dense_ref, node_ref, fold_ref, grad_ref, hess_ref, input_sem,
    level, small, gathered, kinds, meta_ref, rows_of, weight, most_ref, dense_row,
    local_sem, weight_sem, small_send, small_recv, bulk_send, bulk_recv, meta_send, meta_recv, dense_send, dense_recv,
):
    i = lax.axis_index("rows")
    b = lax.axis_index("bundles")
    barrier = pltpu.get_barrier_semaphore()
    for o in range(1, NR):
        pl.semaphore_signal(barrier, inc=1, device_id={"rows": lax.rem(i + o, NR)})
    for o in range(1, NB):
        pl.semaphore_signal(barrier, inc=1, device_id={"bundles": lax.rem(b + o, NB)})
    loads = [
        pltpu.make_async_copy(source, target, input_sem.at[n])
        for n, (source, target) in enumerate(
            (
                (node_hbm, node_ref), (fold_hbm, fold_ref), (grad_hbm, grad_ref), (hess_hbm, hess_ref),
                (dense_hbm, dense_ref), (mask_hbm, mask_ref),
            )
        )
    ]
    piece_rows = bins_ref.shape[0] // PIECES
    bins_loads = [
        pltpu.make_async_copy(
            bins_hbm.at[pl.ds(n * piece_rows, piece_rows)],
            bins_ref.at[pl.ds(n * piece_rows, piece_rows)],
            input_sem.at[6 + n],
        )
        for n in range(PIECES)
    ]
    for load in loads + bins_loads:
        load.start()

    def turn_piece(piece):
        bins_loads[piece].wait()

        def block(t, _):
            rows = pl.ds(pl.multiple_of(t * 128, 128), 128)
            marks = mask_ref[pl.ds(t, 1), :]
            values = jnp.where(marks > 0, bins_ref[rows, :], 0).astype(F32)
            turned = values.T.astype(BF16)
            for s in range(2):
                for p in range(NR):
                    first = s * 128 + p * 16
                    level[s, p, :, rows] = turned[first : first + 16]
            return 0

        blocks = piece_rows // 128
        lax.fori_loop(piece * blocks, (piece + 1) * blocks, block, 0)

    early = pl.ds(0, piece_rows)

    def send_early():
        for o in range(1, NR):
            peer = lax.rem(i + o, NR)
            copy = pltpu.make_async_remote_copy(
                src_ref=level.at[:, peer, :, early], dst_ref=out_ref.at[i],
                send_sem=bulk_send.at[o], recv_sem=bulk_recv.at[o], device_id={"rows": peer},
            )
            copy.start()
            bulk.append(copy)

    for load in loads[:5]:
        load.wait()
    row_data = jnp.concatenate(
        [r[...].astype(F32) for r in (node_ref, fold_ref, grad_ref, hess_ref)], 0
    )
    dense = dense_ref[...].astype(F32)
    for p in range(NR):
        small[p] = jnp.concatenate(
            [row_data, dense[p * PER : (p + 1) * PER], jnp.zeros((12 - PER, 128), F32)], 0
        ).astype(BF16)

    loads[5].wait()
    turn_piece(0)
    pl.semaphore_wait(barrier, NR - 1 + NB - 1)

    copies = []
    for o in range(1, NR):
        peer = lax.rem(i + o, NR)
        copy = pltpu.make_async_remote_copy(
            src_ref=small.at[peer], dst_ref=gathered.at[i],
            send_sem=small_send.at[o], recv_sem=small_recv.at[o], device_id={"rows": peer},
        )
        copy.start()
        copies.append(copy)
    own_small = pltpu.make_async_copy(small.at[i], gathered.at[i], local_sem.at[0])
    own_small.start()

    bulk = []
    send_early()
    own_small.wait()
    for copy in copies:
        copy.wait()
    tiles = [gathered[p].astype(F32) for p in range(NR)]
    lines = [jnp.concatenate([t[n : n + 1] for t in tiles], 0) for n in range(4 + PER)]
    kinds[0] = jnp.concatenate(lines[0:2], 0).astype(BF16)
    kinds[1] = jnp.concatenate(lines[2:4], 0).astype(BF16)
    for n in range(PER):
        kinds[2 + n] = jnp.concatenate([lines[4 + n]] * 2, 0).astype(BF16)
    metas = []
    for o in range(1, NB):
        peer = lax.rem(b + o, NB)
        copy = pltpu.make_async_remote_copy(
            src_ref=kinds.at[0:2], dst_ref=meta_ref.at[b, 0:2],
            send_sem=meta_send.at[o], recv_sem=meta_recv.at[o], device_id={"bundles": peer},
        )
        copy.start()
        metas.append(copy)
        copy = pltpu.make_async_remote_copy(
            src_ref=kinds.at[2 + jnp.minimum(peer, PER - 1)], dst_ref=meta_ref.at[b, 2],
            send_sem=dense_send.at[o], recv_sem=dense_recv.at[o], device_id={"bundles": peer},
        )
        copy.start()
        metas.append(copy)
    own_meta = pltpu.make_async_copy(kinds.at[0:2], meta_ref.at[b, 0:2], local_sem.at[2])
    own_meta.start()
    own_dense = pltpu.make_async_copy(
        kinds.at[2 + jnp.minimum(b, PER - 1)], meta_ref.at[b, 2], local_sem.at[3]
    )
    own_dense.start()
    own_bulk = pltpu.make_async_copy(level.at[:, i, :, early], out_ref.at[i], local_sem.at[1])
    own_bulk.start()
    turn_piece(1)
    late_copy = pltpu.make_async_copy(
        level.at[:, :, :, pl.ds(piece_rows, piece_rows)], late_out, local_sem.at[6]
    )
    late_copy.start()
    own_meta.wait()
    own_dense.wait()
    for copy in metas:
        copy.wait()

    code = lax.broadcasted_iota(jnp.int32, (32, 128), 0)
    node_of = jnp.where(code < PAIRS, code % NODES, -1).astype(F32)
    fold_of = (code // NODES).astype(F32)
    rows = bins_ref.shape[0]

    def weights_out(p):
        lanes = pl.ds(pl.multiple_of(p * rows, rows), rows)
        return pltpu.make_async_copy(weight.at[:, lanes], weight_out.at[:, lanes], weight_sem.at[p])

    for n in range(NB):
        rows_of[n] = meta_ref[n].astype(F32)

    def prepare(p, most):
        first = pl.multiple_of(p * rows, rows)
        for n in range(0, NB, 2):
            signed = size = 0.0
            for m in (n, n + 1):
                lanes = pl.ds(pl.multiple_of(first + m * 128, 128), 128)
                node, fold, grad, hess = (
                    jnp.broadcast_to(rows_of[m, kind, pl.ds(p + line, 1), :], (32, 128))
                    for kind, line in ((0, 0), (0, NR), (1, 0), (1, NR))
                )
                here = node == node_of
                grad = jnp.where(here & (fold != fold_of), grad, 0.0)
                hess = jnp.where(here & (fold == fold_of), hess, 0.0)
                weight[0:32, lanes] = grad.astype(F8)
                weight[32:64, lanes] = hess.astype(F8)
                signed = signed + jnp.where(grad < 0, grad * -4096.0, grad)
                size = size + hess
                dense_row[:, lanes] = rows_of[m, 2, pl.ds(p, 1), :]
            both = jnp.sum(signed, 1, keepdims=True)
            below = jnp.floor(both * (1.0 / 4096.0))
            most = jnp.maximum(most, jnp.maximum(below, both - below * 4096.0))
            most = jnp.maximum(most, jnp.sum(size, 1, keepdims=True))
        weights_out(p).start()
        return most

    most = lax.fori_loop(0, NR, prepare, jnp.zeros((32, 1), F32))
    most_ref[...] = jnp.broadcast_to(jnp.max(most, 0, keepdims=True), (8, 128))
    own_most = pltpu.make_async_copy(most_ref, most_out, local_sem.at[4])
    own_most.start()
    own_best = pltpu.make_async_copy(dense_row, dense_out, local_sem.at[5])
    own_best.start()
    own_bulk.wait()
    late_copy.wait()
    own_most.wait()
    for p in range(NR):
        weights_out(p).wait()
    for copy in bulk:
        copy.wait()
    own_best.wait()


def exchange(bundle_bins, block_mask, dense_bins, row_data):
    anywhere = pl.BlockSpec(memory_space=pl.ANY)
    rows = bundle_bins.shape[0]
    dma = pltpu.SemaphoreType.DMA
    return pl.pallas_call(
        exchange_kernel,
        out_shape=(
            jax.ShapeDtypeStruct((NR, 2, 16, rows // 2), BF16),
            jax.ShapeDtypeStruct((2, NR, 16, rows // 2), BF16),
            jax.ShapeDtypeStruct((64, NR * rows), F8),
            jax.ShapeDtypeStruct((8, 128), F32),
            jax.ShapeDtypeStruct((1, NR * rows), F32),
        ),
        in_specs=[anywhere] * 7,
        out_specs=(anywhere,) * 5,
        scratch_shapes=[
            *(pltpu.VMEM(v.shape, v.dtype) for v in (bundle_bins, block_mask, dense_bins, *row_data)),
            dma((6 + PIECES,)),
            pltpu.VMEM((2, NR, 16, rows), BF16),
            pltpu.VMEM((NR, 16, 128), BF16),
            pltpu.VMEM((NR, 16, 128), BF16),
            pltpu.VMEM((2 + PER, 16, 128), BF16),
            pltpu.VMEM((NB, 3, 16, 128), BF16),
            pltpu.VMEM((NB, 3, 16, 128), F32),
            pltpu.VMEM((64, NR * rows), F8),
            pltpu.VMEM((8, 128), F32),
            pltpu.VMEM((1, NR * rows), F32),
            dma((7,)), dma((NR,)),
            dma((NR,)), dma((NR,)), dma((NR,)), dma((NR,)),
            dma((NB,)), dma((NB,)), dma((NB,)), dma((NB,)),
        ],
        compiler_params=pltpu.CompilerParams(
            collective_id=0, has_side_effects=True, vmem_limit_bytes=VMEM_BYTES
        ),
        name="exchange",
    )(bundle_bins, block_mask, dense_bins, *row_data)


def finish_kernel(
    narrow, level_hbm, late_hbm, weight_hbm, dense_hbm, rows_all, dense_all,
    level_ref, late_ref, weight, dense_row, lev, hist, added, best, dense_best, dense_own,
    sems, send_a, recv_a, send_b, recv_b, send_c, recv_c, send_d, recv_d,
):
    i = lax.axis_index("rows")
    b = lax.axis_index("bundles")
    half = level_ref.shape[3]
    total = NR * 2 * half
    chunk = 1024
    dtype = F8 if narrow else BF16
    loads = [
        pltpu.make_async_copy(source, target, sems.at[n])
        for n, (source, target) in enumerate(
            ((dense_hbm, dense_row), (weight_hbm, weight), (level_hbm, level_ref))
        )
    ]
    for load in loads:
        load.start()
    barrier = pltpu.get_barrier_semaphore()
    for o in range(1, NR):
        pl.semaphore_signal(barrier, inc=1, device_id={"rows": lax.rem(i + o, NR)})
    for o in range(1, NB):
        pl.semaphore_signal(barrier, inc=1, device_id={"bundles": lax.rem(b + o, NB)})

    def feature(source, j, starts):
        acc = None
        for start in starts:
            for k in range(start, start + half, chunk):
                w = weight[:, k : k + chunk].astype(dtype)
                part = sums_of(source[pl.ds(j, 1), k : k + chunk].astype(BF16), w, dtype)
                acc = part if acc is None else acc + part
        return acc

    early_starts = range(0, total, 2 * half)
    late_starts = range(half, total, 2 * half)

    def across(source, peer):
        return pltpu.make_async_remote_copy(
            src_ref=dense_best, dst_ref=dense_own.at[source],
            send_sem=send_a.at[peer], recv_sem=recv_a.at[source], device_id={"bundles": peer},
        )

    def own_across(source):
        return pltpu.make_async_copy(dense_best, dense_own.at[source], sems.at[3])

    def along(o, source, target, send, recv):
        return pltpu.make_async_remote_copy(
            src_ref=source, dst_ref=target.at[i],
            send_sem=send.at[o], recv_sem=recv.at[o], device_id={"rows": lax.rem(i + o, NR)},
        )

    def late(o):
        peer = lax.rem(i + o, NR)
        return pltpu.make_async_remote_copy(
            src_ref=late_hbm.at[:, peer], dst_ref=late_ref.at[i],
            send_sem=send_d.at[o], recv_sem=recv_d.at[o], device_id={"rows": peer},
        )

    own_late = pltpu.make_async_copy(late_hbm.at[:, i], late_ref.at[i], sems.at[6])
    own_late.start()

    def spread_from(ref, offset):
        def spread(p, _):
            lanes = pl.ds(pl.multiple_of(p * (2 * half) + offset, half), half)
            lev[0:16, lanes] = ref[p, 0].astype(F32)
            lev[16:32, lanes] = ref[p, 1].astype(F32)
            return 0

        lax.fori_loop(0, NR, spread, 0)

    loads[0].wait()
    loads[1].wait()
    hist[32] = feature(dense_row, 0, range(0, total, half))
    loads[2].wait()
    spread_from(level_ref, 0)

    def first_half(q, _):
        @pl.when(q == 2)
        def _():
            pl.semaphore_wait(barrier, NR - 1 + NB - 1)
            for o in range(1, NR):
                late(o).start()
            dense_best[...] = jnp.broadcast_to(best[15:16, :], (8, 128))

        @pl.when(q == 3)
        def _():
            for source in range(PER):
                @pl.when(b == source)
                def _():
                    for peer in range(NB):
                        if peer != source:
                            across(source, peer).start()
                    own_across(source).start()

        best[15:16, :] = best_of(hist[32], hist[32])
        sums = [feature(lev, q + 8 * n, early_starts) for n in range(4)]
        for n in range(4):
            hist[q + 8 * n] = sums[n]
        return 0

    lax.fori_loop(0, 8, first_half, 0)
    own_late.wait()
    for o in range(1, NR):
        late(o).wait()
    spread_from(late_ref, half)

    def gains_of(q):
        sums = [hist[q + 8 * n] + added[n] for n in range(4)]
        best[pl.ds(q, 1), :] = best_of(sums[0], sums[2])
        best[pl.ds(q + 8, 1), :] = best_of(sums[1], sums[3])

    added[...] = jnp.zeros_like(added)

    def second_half(q, _):
        @pl.when(q == 2)
        def _():
            for source in range(PER):
                @pl.when(b == source)
                def _():
                    own_across(source).wait()
                    for peer in range(NB):
                        if peer != source:
                            across(source, peer).wait_send()

                @pl.when(b != source)
                def _():
                    across(source, 0).wait_recv()
            for o in range(1, NR):
                along(o, dense_own, dense_all, send_c, recv_c).start()
            pltpu.make_async_copy(dense_own, dense_all.at[i], sems.at[4]).start()

        old = jnp.maximum(q - 1, 0)
        gains_of(old)
        sums = [feature(lev, q + 8 * n, late_starts) for n in range(4)]
        for n in range(4):
            added[n] = sums[n]
        return 0

    lax.fori_loop(0, 8, second_half, 0)
    gains_of(7)

    pltpu.make_async_copy(dense_own, dense_all.at[i], sems.at[4]).wait()
    for o in range(1, NR):
        along(o, dense_own, dense_all, send_c, recv_c).wait()
    for o in range(1, NR):
        along(o, best, rows_all, send_b, recv_b).start()
    own = pltpu.make_async_copy(best, rows_all.at[i], sems.at[5])
    own.start()
    own.wait()
    for o in range(1, NR):
        along(o, best, rows_all, send_b, recv_b).wait()


def finish(narrow, level, late, weight, dense):
    anywhere = pl.BlockSpec(memory_space=pl.ANY)
    dma = pltpu.SemaphoreType.DMA
    return pl.pallas_call(
        functools.partial(finish_kernel, narrow),
        out_shape=(
            jax.ShapeDtypeStruct((NR, 16, 128), F32),
            jax.ShapeDtypeStruct((NR, PER, 8, 128), F32),
        ),
        in_specs=[anywhere] * 4,
        out_specs=(anywhere, anywhere),
        scratch_shapes=[
            pltpu.VMEM(level.shape, BF16),
            pltpu.VMEM(level.shape, BF16),
            pltpu.VMEM(weight.shape, F8),
            pltpu.VMEM(dense.shape, F32),
            pltpu.VMEM((32, weight.shape[1]), F32),
            pltpu.VMEM((33, 128, 128), F32),
            pltpu.VMEM((4, 128, 128), F32),
            pltpu.VMEM((16, 128), F32),
            pltpu.VMEM((8, 128), F32),
            pltpu.VMEM((PER, 8, 128), F32),
            dma((7,)), dma((NB,)), dma((PER,)), *(dma((NR,)) for _ in range(6)),
        ],
        compiler_params=pltpu.CompilerParams(
            collective_id=1 if narrow else 2, has_side_effects=True, vmem_limit_bytes=VMEM_BYTES
        ),
        name="finish8" if narrow else "finish16",
    )(level, late, weight, dense)


def assemble_kernel(rows_ref, dense_ref, bundle_out, dense_out):
    turned = rows_ref[...].reshape(NR * 16, 128).T
    pieces = [dense_ref[r, d, 0:1, :] for r in range(NR) for d in range(PER)]
    dense = jnp.concatenate(pieces + [jnp.zeros((128 - DENSE, 128), F32)], 0).T
    for k in range(FOLDS):
        nodes = slice(k * NODES, (k + 1) * NODES)
        bundle_out[k, :, 0:128] = turned[nodes]
        bundle_out[k, :, 128:256] = turned[32:64][nodes]
        dense_out[k] = dense[nodes, 0:DENSE]


def assemble(rows_all, dense_all):
    return pl.pallas_call(
        assemble_kernel,
        out_shape=(
            jax.ShapeDtypeStruct((FOLDS, NODES, 256), F32),
            jax.ShapeDtypeStruct((FOLDS, NODES, DENSE), F32),
        ),
        name="assemble",
    )(rows_all, dense_all)


def local(dense_bins, bundle_bins, block_mask, node_ids, fold_ids, grads, hessians):
    row_data = [v.reshape(1, -1) for v in (node_ids, fold_ids, grads, hessians)]
    level, late, weight, most, dense = exchange(bundle_bins, block_mask, dense_bins, row_data)
    rows_all, dense_all = lax.cond(
        most[0, 0] <= EXACT,
        functools.partial(finish, True), functools.partial(finish, False),
        level, late, weight, dense,
    )
    return assemble(rows_all, dense_all)


def solution(mesh):
    placed = (
        P(None, ("rows", "bundles")),
        P("rows", "bundles"),
        P("rows", "bundles"),
        P(("rows", "bundles")),
        P(("rows", "bundles")),
        P(("rows", "bundles")),
        P(("rows", "bundles")),
    )
    return jax.shard_map(
        local,
        mesh=mesh,
        in_specs=placed,
        out_specs=(P(None, None, "bundles"), P()),
        check_vma=False,
    )
```
